32 devices in a mesh: member: 2 (over x), lat: 16 (over z, y, core).
Axes of the slice: x: 2, y: 2, z: 4, core: 2. Of those that a mesh axis runs over, the one named last changes fastest.
Arguments:
- state: float32 [10, 128, 128, 256], P('member', None, 'lat'), parts along dimension 0, may hold values from -6 to 6
- wind: float32 [256, 128, 256], P('member', 'lat'), parts along dimension 0, may hold values from -0.9 to 0.9
- sunlight: float32 [256, 256], P(('member', 'lat')), parts along dimension 0, may hold values from 0.1 to 1
- day_list: int32 [32, 16], P(('member', 'lat')), parts along dimension 0, may hold values from -1 to 15, as said below
- w_first: bfloat16 [640, 2048], replicated, may hold values from -0.25 to 0.25
- bias: float32 [2048], replicated, may hold values from -3 to 3
- w_second: bfloat16 [2048, 128], replicated, may hold values from -0.125 to 0.125
- remap: float32 [128, 128], replicated, may hold values from -1.5 to 2
Outputs:
- new_state: float32 [10, 128, 128, 256], P('member', None, 'lat'), parts along dimension 0
The draws below stay inside these ranges and needn't reach their ends.
There are 2 independent parts, one for each index of `member`. The reference program is written for one: setup_inputs(seed, part) draws one part's arguments, and reference() takes and returns one part's arrays. A program takes and returns all parts, laid end to end along the dimension named above; an argument that names none is the same for every part. Nothing has to cross between parts.
Inputs may be any that keep to these rules, and one draw needn't show every extreme that they name: `day_list`: row d names the daylit blocks of band d, each once, as a cyclic run of consecutive numbers placed first, then -1; every row names at least one block. Rows d and d + 8 together name at most 20 blocks; row 0 names all 16 and row 8 exactly 4.
All inputs are finite; a program needn't handle non-finite values.
Results may differ from the reference program's by a relative error of at most 0.00062.
Values may be sent and summed in bfloat16 or wider, within the bound.
No kernel may reach another device: no remote copies, remote signals or barrier semaphores. Data moves between devices by JAX's collectives and lax.ppermute only.
A program may use at most 128 MiB of HBM per device.

```python
import math
import jax
import jax.numpy as jnp
from jax import lax

FIELDS = 5
LEV = 128
HID = 2048
NLON = 256
COLBLK = 128
STEPS = 2
BANDS = 16
NLAT = 128
BLK_DEV = 16


def draw_day_list(key, part):
    half = BANDS // 2
    band = jnp.arange(half, dtype=jnp.int32)
    key_a, key_b, key_c = jax.random.split(key, 3)
    north_cut = jax.random.randint(key_a, (half,), 0, 2, dtype=jnp.int32)
    south_cut = jax.random.randint(key_b, (half,), 0, 2, dtype=jnp.int32)
    north_cut = jnp.where(band == 0, 0, north_cut)
    south_cut = jnp.where(band == 0, 0, south_cut)
    north_less = jnp.minimum(BLK_DEV // 2, band * BLK_DEV // BANDS + north_cut)
    north_count = BLK_DEV - north_less
    south_count = BLK_DEV // 4 + north_less - south_cut
    south_count = jnp.maximum(south_count, 1)
    counts = jnp.concatenate([north_count, south_count])
    starts = jax.random.randint(key_c, (BANDS,), 0, BLK_DEV, dtype=jnp.int32)
    position = jnp.arange(BLK_DEV, dtype=jnp.int32)
    listed = (starts[:, None] + position[None, :]) % BLK_DEV
    return jnp.where(position[None, :] < counts[:, None], listed, -1).astype(jnp.int32)


def draw_remap(key, part):
    noise = jax.random.normal(key, (LEV, LEV), jnp.float32) * (0.5 / math.sqrt(LEV))
    return 0.7 * jnp.eye(LEV, dtype=jnp.float32) + noise


def block_scale(rng, extent, cuts, low, top_value):
    level, own = 1.0, jax.random.fold_in(rng, 6)
    for dim, shards_of in cuts:
        draws = jnp.exp(jax.random.uniform(jax.random.fold_in(own, dim), (shards_of,), jnp.float32, low / len(cuts), top_value / len(cuts)))
        level = level * jnp.repeat(draws, extent[dim] // shards_of).reshape([-1 if axis == dim else 1 for axis in range(len(extent))])
    return level


def scatter_about(stream_key, dims, deviation, reach, pieces=(), kind=jnp.bfloat16):
    values = deviation * jax.random.normal(stream_key, dims, jnp.float32)
    if pieces:
        values = values * block_scale(stream_key, dims, pieces, -0.22, 0.18)
    return jnp.clip(values, -reach, reach).astype(kind)


def setup_inputs(seed: int = 0, part: int = 0) -> dict:
    streams_of = jax.random.split(jax.random.key(seed), 9)
    part_keys = jax.random.split(jax.random.fold_in(streams_of[8], part), 9)
    state = scatter_about(part_keys[0], (FIELDS, LEV, NLAT, NLON), 1.0, 6.0, ((2, 16),), jnp.float32)
    wind = jnp.clip(jax.random.uniform(part_keys[1], (LEV, NLAT, NLON), jnp.float32, -0.9, 0.9) * block_scale(part_keys[1], (LEV, NLAT, NLON), ((1, 16),), -0.4, 0.0), -0.9, 0.9)
    sunlight = jnp.clip(0.1 + 0.9 * jax.random.uniform(part_keys[2], (NLAT, NLON), jnp.float32) ** block_scale(part_keys[2], (NLAT, NLON), ((0, 16),), -0.2, 0.2), 0.1, 1.0)
    day_list = draw_day_list(jax.random.fold_in(jax.random.fold_in(streams_of[8], part), 71), part)
    w_first = scatter_about(streams_of[4], (FIELDS * LEV, HID), (FIELDS * LEV) ** -0.5, 0.25)
    bias = scatter_about(streams_of[5], (HID,), 0.5, 3.0, (), jnp.float32)
    w_second = scatter_about(streams_of[6], (HID, LEV), HID ** -0.5, 0.125)
    remap = draw_remap(jax.random.fold_in(streams_of[8], 71), part)
    return dict(state=state, wind=wind, sunlight=sunlight, day_list=day_list, w_first=w_first, bias=bias, w_second=w_second, remap=remap)


def min_mod(left, right):
    return 0.5 * (jnp.sign(left) + jnp.sign(right)) * jnp.minimum(jnp.abs(left), jnp.abs(right))


def advance(padded, courant):
    length = padded.shape[2] - 4
    slopes = min_mod(padded[:, :, 2:] - padded[:, :, 1:-1], padded[:, :, 1:-1] - padded[:, :, :-2])
    upper_q = padded[:, :, 1:length + 2]
    upper_s = slopes[:, :, 0:length + 1]
    lower_q = padded[:, :, 2:length + 3]
    lower_s = slopes[:, :, 1:length + 2]
    speed = courant[None]
    fluxes = jnp.where(speed > 0.0, speed * (upper_q + 0.5 * (1.0 - speed) * upper_s), speed * (lower_q - 0.5 * (1.0 + speed) * lower_s))
    return padded[:, :, 2:length + 2] - (fluxes[:, :, 1:] - fluxes[:, :, :-1])


def reference(state, wind, sunlight, day_list, w_first, bias, w_second, remap):
    current = state
    courant = jnp.concatenate([wind, jnp.zeros_like(wind[:, :1])], axis=1)
    for step in range(STEPS):
        padded = jnp.pad(current, ((0, 0), (0, 0), (2, 2), (0, 0)))
        current = advance(padded, courant)
    columns = current.reshape(FIELDS, LEV, NLAT * NLON)
    remapped = jnp.einsum("km,fmc->fkc", remap, columns, precision=lax.Precision.HIGHEST)
    inputs = remapped.astype(jnp.bfloat16).reshape(FIELDS, LEV, NLAT, NLON)
    rows_first = jnp.moveaxis(inputs, 2, 0)
    w_shaped = w_first.astype(jnp.float32).reshape(FIELDS, LEV, HID)
    w_out = w_second.astype(jnp.float32)

    def one_row(row):
        hidden = jnp.einsum("flc,flh->ch", row.astype(jnp.float32), w_shaped, precision=lax.Precision.HIGHEST) + bias
        hidden = jax.nn.gelu(hidden, approximate=True).astype(jnp.bfloat16)
        return jnp.dot(hidden.astype(jnp.float32), w_out, precision=lax.Precision.HIGHEST).T

    net = lax.map(one_row, rows_first)
    daylit = jnp.any(day_list[:, None, :] == jnp.arange(BLK_DEV, dtype=jnp.int32)[None, :, None], axis=2)
    daylit = jnp.repeat(daylit.astype(jnp.float32), COLBLK, axis=1).reshape(NLAT, NLON)
    heating = jnp.moveaxis(net, 1, 0) * (daylit * sunlight)[None]
    heating = heating.reshape(1, LEV, NLAT * NLON)
    output = jnp.concatenate([remapped[:1] + heating, remapped[1:]], axis=0)
    return output.reshape(FIELDS, LEV, NLAT, NLON)
```

```python
import functools
import jax
import jax.numpy as jnp
from jax import lax
from jax.experimental import pallas as pl
from jax.experimental.pallas import tpu as pltpu
from jax.sharding import PartitionSpec as P

LANES = 128
KB = 32
GELU_A = 0.7978845608028654
GELU_B = 0.7978845608028654 * 0.044715
ANY = pl.BlockSpec(memory_space=pl.ANY)


def limited(ahead, behind):
    return jnp.maximum(jnp.minimum(ahead, jnp.maximum(behind, 0.0)), jnp.minimum(behind, 0.0))


def face(speed):
    size = jnp.abs(speed)
    return speed > 0.0, speed, size * (0.5 - 0.5 * size)


def rows_after(q, faces):
    diffs = [b - a for a, b in zip(q[:-1], q[1:])]
    slopes = [None] + [limited(b, a) for a, b in zip(diffs[:-1], diffs[1:])]
    fluxes = []
    for j, (mask, speed, half) in enumerate(faces):
        edge = jnp.where(mask, q[j + 1], q[j + 2])
        slope = jnp.where(mask, slopes[j + 1], slopes[j + 2])
        fluxes.append(speed * edge + half * slope)
    return [q[j + 2] - (fluxes[j + 1] - fluxes[j]) for j in range(len(faces) - 1)]


def row_of(ref, start, count, rows):
    return ref[pl.ds(start, count, stride=rows), :]


def pack_kernel(state_ref, wind_ref, up_ref, down_ref):
    fields, levels, rows, lanes = state_ref.shape
    flat = state_ref.reshape(fields * levels * rows, lanes)
    winds = wind_ref.reshape(levels * rows, lanes)
    for f in range(fields):
        for r in range(2):
            first = row_of(flat, f * levels * rows + r, levels, rows)
            down_ref[0, r * fields + f] = first.astype(jnp.bfloat16)
            last = row_of(flat, f * levels * rows + rows - 2 + r, levels, rows)
            up_ref[0, r * fields + f] = last.astype(jnp.bfloat16)
    speed = row_of(winds, 0, levels, rows)
    high = speed.astype(jnp.bfloat16)
    down_ref[0, 2 * fields] = high
    down_ref[0, 2 * fields + 1] = (speed - high.astype(jnp.float32)).astype(jnp.bfloat16)


def pack(state, wind):
    fields, levels, rows, lons = state.shape
    halves = lons // LANES
    return pl.pallas_call(
        pack_kernel,
        grid=(halves, levels // KB),
        in_specs=[
            pl.BlockSpec((fields, KB, rows, LANES), lambda h, k: (0, k, 0, h)),
            pl.BlockSpec((KB, rows, LANES), lambda h, k: (k, 0, h)),
        ],
        out_specs=[
            pl.BlockSpec((1, 2 * fields, KB, LANES), lambda h, k: (h, 0, k, 0)),
            pl.BlockSpec((1, 2 * fields + 2, KB, LANES), lambda h, k: (h, 0, k, 0)),
        ],
        out_shape=[
            jax.ShapeDtypeStruct((halves, 2 * fields, levels, LANES), jnp.bfloat16),
            jax.ShapeDtypeStruct((halves, 2 * fields + 2, levels, LANES), jnp.bfloat16),
        ],
        name="pack",
    )(state, wind)


def inner_kernel(state_ref, wind_ref, out_ref):
    fields, levels, rows, lanes = state_ref.shape
    flat = state_ref.reshape(fields * levels * rows, lanes)
    winds = wind_ref.reshape(levels * rows, lanes)
    step = 8

    @pl.loop(0, levels // step)
    def _(i):
        base = i * (step * rows)
        faces = [face(row_of(winds, base + r, step, rows)) for r in range(2, rows - 1)]
        level = pl.multiple_of(i * step, step)
        for f in range(fields):
            q = [row_of(flat, f * levels * rows + base + r, step, rows) for r in range(rows)]
            for r, value in enumerate(rows_after(q, faces)):
                out_ref[0, r, f, pl.ds(level, step), :] = value


def inner(state, wind):
    fields, levels, rows, lons = state.shape
    halves = lons // LANES
    return pl.pallas_call(
        inner_kernel,
        grid=(halves, levels // KB),
        in_specs=[
            pl.BlockSpec((fields, KB, rows, LANES), lambda h, k: (0, k, 0, h)),
            pl.BlockSpec((KB, rows, LANES), lambda h, k: (k, 0, h)),
        ],
        out_specs=pl.BlockSpec((1, rows - 4, fields, KB, LANES), lambda h, k: (h, 0, 0, k, 0)),
        out_shape=jax.ShapeDtypeStruct((halves, rows - 4, fields, levels, LANES), jnp.float32),
        cost_estimate=pl.CostEstimate(flops=100_000_000, bytes_accessed=8_000_000, transcendentals=0),
        name="inner",
    )(state, wind)


def edge_kernel(state_ref, wind_ref, above_ref, below_ref, out_ref, up_ref, down_ref):
    fields, levels, rows, lanes = state_ref.shape
    flat = state_ref.reshape(fields * levels * rows, lanes)
    winds = wind_ref.reshape(levels * rows, lanes)
    step = 16

    @pl.loop(0, levels // step)
    def _(i):
        base = i * (step * rows)
        level = pl.multiple_of(i * step, step)
        here = pl.ds(level, step)
        wide = lambda ref, index: ref[0, index, here, :].astype(jnp.float32)
        speeds = {r: row_of(winds, base + r, step, rows) for r in (0, 1, 2, rows - 2, rows - 1)}
        speeds[rows] = wide(below_ref, 2 * fields) + wide(below_ref, 2 * fields + 1)
        for side, first in enumerate((0, rows - 2)):
            faces = [face(speeds[first + j]) for j in range(3)]
            for f in range(fields):
                own = lambda r: row_of(flat, f * levels * rows + base + r, step, rows)
                if side == 0:
                    q = [wide(above_ref, f), wide(above_ref, fields + f)] + [own(r) for r in range(4)]
                else:
                    q = [own(r) for r in range(rows - 4, rows)] + [wide(below_ref, f), wide(below_ref, fields + f)]
                sent = (down_ref, up_ref)[side]
                for r, value in enumerate(rows_after(q, faces)):
                    out_ref[0, 2 * side + r, f, here, :] = value
                    sent[0, r * fields + f, here, :] = value.astype(jnp.bfloat16)


def edge(state, wind, above, below):
    fields, levels, rows, lons = state.shape
    halves = lons // LANES
    sent = pl.BlockSpec((1, 2 * fields, KB, LANES), lambda h, k: (h, 0, k, 0))
    return pl.pallas_call(
        edge_kernel,
        grid=(halves, levels // KB),
        in_specs=[
            pl.BlockSpec((fields, KB, rows, LANES), lambda h, k: (0, k, 0, h)),
            pl.BlockSpec((KB, rows, LANES), lambda h, k: (k, 0, h)),
            sent,
            pl.BlockSpec((1, 2 * fields + 2, KB, LANES), lambda h, k: (h, 0, k, 0)),
        ],
        out_specs=[
            pl.BlockSpec((1, 4, fields, KB, LANES), lambda h, k: (h, 0, 0, k, 0)),
            sent,
            sent,
        ],
        out_shape=[
            jax.ShapeDtypeStruct((halves, 4, fields, levels, LANES), jnp.float32),
            jax.ShapeDtypeStruct((halves, 2 * fields, levels, LANES), jnp.bfloat16),
            jax.ShapeDtypeStruct((halves, 2 * fields, levels, LANES), jnp.bfloat16),
        ],
        cost_estimate=pl.CostEstimate(flops=100_000_000, bytes_accessed=10_000_000, transcendentals=0),
        name="edge",
    )(state, wind, above, below)


def weights_kernel(first_ref, bias_ref, second_ref, remap_ref, first_out, second_out, split_out):
    inputs, units = first_ref.shape
    levels = remap_ref.shape[0]
    whole = remap_ref[...]
    r_high = whole.astype(jnp.bfloat16)
    r_low = (whole - r_high.astype(jnp.float32)).astype(jnp.bfloat16)
    for j in range(2):
        split_out[:levels, j * levels : (j + 1) * levels] = r_high
        split_out[levels:, j * levels : (j + 1) * levels] = r_low
    wide = first_ref[...].astype(jnp.float32)
    for j in range(inputs // LANES):
        part = wide[j * LANES : (j + 1) * LANES]
        first_out[:, j * LANES : (j + 1) * LANES] = part.T.astype(jnp.bfloat16)
    bias = bias_ref[...]
    high = bias.astype(jnp.bfloat16).astype(jnp.float32)
    middle = (bias - high).astype(jnp.bfloat16).astype(jnp.float32)
    low = bias - high - middle
    row = lax.broadcasted_iota(jnp.int32, (LANES, units), 0)
    stacked = jnp.where(row == 0, high, jnp.where(row == 1, middle, jnp.where(row == 2, low, 0.0)))
    first_out[:, inputs:] = stacked.T.astype(jnp.bfloat16)
    second_out[...] = second_ref[...].astype(jnp.float32).T.astype(jnp.bfloat16)


def weights(w_first, bias, w_second, remap):
    inputs, hidden = w_first.shape
    levels = remap.shape[0]
    outputs = w_second.shape[1]
    return pl.pallas_call(
        weights_kernel,
        grid=(hidden // LANES,),
        in_specs=[
            pl.BlockSpec((inputs, LANES), lambda i: (0, i)),
            pl.BlockSpec((1, LANES), lambda i: (0, i)),
            pl.BlockSpec((LANES, outputs), lambda i: (i, 0)),
            pl.BlockSpec((levels, levels), lambda i: (0, 0)),
        ],
        out_specs=[
            pl.BlockSpec((LANES, inputs + LANES), lambda i: (i, 0)),
            pl.BlockSpec((outputs, LANES), lambda i: (0, i)),
            pl.BlockSpec((2 * levels, 2 * levels), lambda i: (0, 0)),
        ],
        out_shape=[
            jax.ShapeDtypeStruct((hidden, inputs + LANES), jnp.bfloat16),
            jax.ShapeDtypeStruct((outputs, hidden), jnp.bfloat16),
            jax.ShapeDtypeStruct((2 * levels, 2 * levels), jnp.bfloat16),
        ],
        cost_estimate=pl.CostEstimate(flops=100_000_000, bytes_accessed=7_000_000, transcendentals=0),
        name="weights",
    )(w_first, bias.reshape(1, hidden), w_second, remap)


def network(x, w1_ref, w2_ref):
    hidden = w1_ref.shape[0]
    chunk = 256
    total = None
    for c in range(hidden // chunk):
        v = jnp.dot(w1_ref[c * chunk : (c + 1) * chunk, :], x, preferred_element_type=jnp.float32)
        h = 0.5 * v
        t = jnp.tanh(v * (GELU_A + GELU_B * (v * v)))
        g = (h + h * t).astype(jnp.bfloat16)
        part = jnp.dot(w2_ref[:, c * chunk : (c + 1) * chunk], g, preferred_element_type=jnp.float32)
        total = part if total is None else total + part
    return total


def finish_kernel(edges, halves, *refs):
    if edges:
        (mid_hbm, edge_hbm, wind_hbm, scale_hbm, rcat_hbm, w1_hbm, w2_hbm, above_hbm, below_hbm, first_hbm, old_hbm,
         out_hbm, mid, edg, wnd, scale, rcat, w1, w2, a, x, rem, out, above, below, last, sems) = refs
    else:
        (mid_hbm, edge_hbm, wind_hbm, scale_hbm, rcat_hbm, w1_hbm, w2_hbm,
         out_hbm, mid, edg, wnd, scale, rcat, w1, w2, a, x, rem, out, sems) = refs
    count = len(halves)
    fields, levels, rows = out.shape[1:4]
    counter = iter(range(sems.shape[0]))

    def copy(source, target):
        made = pltpu.make_async_copy(source, target, sems.at[next(counter)])
        made.start()
        return made

    loads = []
    for s, h in enumerate(halves):
        lon = pl.ds(h * LANES, LANES)
        pending = [
            copy(mid_hbm.at[h], mid.at[s]),
            copy(edge_hbm.at[h], edg.at[s]),
            copy(wind_hbm.at[:, :, lon], wnd.at[s]),
        ]
        if edges:
            pending += [
                copy(above_hbm.at[h], above.at[s]),
                copy(below_hbm.at[h], below.at[s]),
                copy(first_hbm.at[h, pl.ds(2 * fields, 2)], last.at[s]),
            ]
        loads.append(pending)
        if s == 0:
            small = [copy(rcat_hbm, rcat), copy(scale_hbm, scale)]
            heavy = [copy(w1_hbm, w1), copy(w2_hbm, w2)]
    olds = []
    if edges:
        for s, h in enumerate(halves):
            olds.append(copy(old_hbm.at[:, :, :, pl.ds(h * LANES, LANES)], out.at[s]))

    inputs = fields * levels
    row = lax.broadcasted_iota(jnp.int32, (x.shape[1] - inputs, x.shape[2]), 0)
    for u in range(2):
        x[u, inputs:, :] = jnp.where(row < 3, 1.0, 0.0).astype(jnp.bfloat16)

    step = 16
    stores = []
    for s, h in enumerate(halves):
        for made in loads[s]:
            made.wait()
        winds = wnd.at[s].reshape(levels * rows, LANES)

        @pl.loop(0, levels // step)
        def _(i):
            here = pl.ds(pl.multiple_of(i * step, step), step)
            there = pl.ds(pl.multiple_of(levels + i * step, step), step)
            base = i * (step * rows)
            if edges:
                wide = lambda ref, index: ref[s, index, here, :].astype(jnp.float32)
                needed = (0, 1, 2, rows - 2, rows - 1)
                speeds = {r: row_of(winds, base + r, step, rows) for r in needed}
                speeds[rows] = wide(last, 0) + wide(last, 1)
                groups = ((0, 2), (rows - 2, 2))
            else:
                speeds = {r: row_of(winds, base + r, step, rows) for r in range(2, rows - 1)}
                groups = ((2, 4),)
            for first, many in groups:
                faces = [face(speeds[first + j]) for j in range(many + 1)]
                for f in range(fields):
                    kept = lambda r: (mid[s, r - 2, f, here, :] if 2 <= r < rows - 2 else
                                      edg[s, r if r < 2 else r - rows + 4, f, here, :])
                    q = []
                    for r in range(first - 2, first + many + 2):
                        if r < 0:
                            q.append(wide(above, (r + 2) * fields + f))
                        elif r >= rows:
                            q.append(wide(below, (r - rows) * fields + f))
                        else:
                            q.append(kept(r))
                    for j, value in enumerate(rows_after(q, faces)):
                        if edges:
                            u, place = (0 if first == 0 else 1), j
                        else:
                            u, place = j // 2, j % 2
                        cols = pl.ds(place * LANES, LANES)
                        high = value.astype(jnp.bfloat16)
                        a[u, f, here, cols] = high
                        a[u, f, there, cols] = (value - high.astype(jnp.float32)).astype(jnp.bfloat16)

        if s == 0:
            for made in small:
                made.wait()
        if edges:
            olds[s].wait()
        flat = out.at[s].reshape(fields * levels * rows, LANES)
        starts = (0, rows - 2) if edges else (2, 4)
        for u in range(2):
            for f in range(fields):
                both = jnp.dot(rcat[...], a[u, f], preferred_element_type=jnp.float32)
                value = both[:levels] + both[levels:]
                x[u, f * levels : (f + 1) * levels, :] = value.astype(jnp.bfloat16)
                if f == 0:
                    rem[u] = value
                else:
                    for place in range(2):
                        flat[pl.ds(f * levels * rows + starts[u] + place, levels, stride=rows), :] = (
                            value[:, place * LANES : (place + 1) * LANES])
        lon = pl.ds(h * LANES, LANES)
        stores.append(copy(out.at[s, pl.ds(1, fields - 1)], out_hbm.at[pl.ds(1, fields - 1), :, :, lon]))
        if s == 0:
            for made in heavy:
                made.wait()

        for u in range(2):
            net = network(x[u], w1, w2)
            for place in range(2):
                r = starts[u] + place
                part = slice(place * LANES, (place + 1) * LANES)
                light = scale[r : r + 1, h * LANES : (h + 1) * LANES]
                flat[pl.ds(r, levels, stride=rows), :] = rem[u, :, part] + net[:, part] * light
        stores.append(copy(out.at[s, 0], out_hbm.at[0, :, :, lon]))
    for made in stores:
        made.wait()


def finish(edges, halves, mid, edge_rows, wind, scale, rcat, w1, w2, *more):
    total_halves, inner_rows, fields, levels, _ = mid.shape
    rows = inner_rows + 4
    lons = total_halves * LANES
    n = len(halves)
    f32, b16 = jnp.float32, jnp.bfloat16
    scratch = [
        pltpu.VMEM((n,) + mid.shape[1:], f32),
        pltpu.VMEM((n,) + edge_rows.shape[1:], f32),
        pltpu.VMEM((n, levels, rows, LANES), f32),
        pltpu.VMEM(scale.shape, f32),
        pltpu.VMEM(rcat.shape, b16),
        pltpu.VMEM(w1.shape, b16),
        pltpu.VMEM(w2.shape, b16),
        pltpu.VMEM((2, fields, 2 * levels, 2 * LANES), b16),
        pltpu.VMEM((2, w1.shape[1], 2 * LANES), b16),
        pltpu.VMEM((2, levels, 2 * LANES), f32),
        pltpu.VMEM((n, fields, levels, rows, LANES), f32),
    ]
    semaphores = 4 + 5 * n
    if edges:
        scratch += [
            pltpu.VMEM((n, 2 * fields, levels, LANES), b16),
            pltpu.VMEM((n, 2 * fields, levels, LANES), b16),
            pltpu.VMEM((n, 2, levels, LANES), b16),
        ]
        semaphores += 4 * n
    scratch.append(pltpu.SemaphoreType.DMA((semaphores,)))
    operands = (mid, edge_rows, wind, scale, rcat, w1, w2) + more
    return pl.pallas_call(
        functools.partial(finish_kernel, edges, halves),
        in_specs=[ANY] * len(operands),
        out_specs=ANY,
        out_shape=jax.ShapeDtypeStruct((fields, levels, rows, lons), f32),
        scratch_shapes=scratch,
        input_output_aliases={len(operands) - 1: 0} if edges else {},
        compiler_params=pltpu.CompilerParams(vmem_limit_bytes=44 * 1024 * 1024),
        cost_estimate=pl.CostEstimate(flops=4_000_000_000, bytes_accessed=12_000_000, transcendentals=2_000_000),
        name="finish_edges" if edges else "finish_inner",
    )(*operands)


def shards(state, wind, sunlight, day_list, w_first, bias, w_second, remap):
    fields, levels, rows, lons = state.shape
    halves = lons // LANES
    count = lax.axis_size("lat")
    forward = [(i, i + 1) for i in range(count - 1)]
    back = [(i + 1, i) for i in range(count - 1)]
    up, down = pack(state, wind)
    above = lax.ppermute(up, "lat", forward)
    below = lax.ppermute(down, "lat", back)

    mid = inner(state, wind)
    w1, w2, rcat = weights(w_first, bias, w_second, remap)
    blocks = day_list.shape[1]
    lit = jnp.any(day_list[0][None, :] == jnp.arange(blocks, dtype=jnp.int32)[:, None], axis=1)
    lit = jnp.broadcast_to(lit.astype(jnp.float32).reshape(rows, halves, 1), (rows, halves, LANES))
    scale = sunlight * lit.reshape(rows, lons)

    edge_rows, up2, down2 = edge(state, wind, above, below)
    above2 = lax.ppermute(up2, "lat", forward)
    below2 = lax.ppermute(down2, "lat", back)
    every = tuple(range(halves))
    partial = finish(False, every, mid, edge_rows, wind, scale, rcat, w1, w2)
    return finish(True, every, mid, edge_rows, wind, scale, rcat, w1, w2, above2, below2, below, partial)


def solution(mesh):
    placed = (
        P("member", None, "lat", None),
        P("member", "lat", None),
        P(("member", "lat"), None),
        P(("member", "lat"), None),
        P(),
        P(),
        P(),
        P(),
    )
    return jax.shard_map(
        shards,
        mesh=mesh,
        in_specs=placed,
        out_specs=P("member", None, "lat", None),
        check_vma=False,
    )
```

```python
import functools
import jax
import jax.numpy as jnp
from jax import lax
from jax.experimental import pallas as pl
from jax.experimental.pallas import tpu as pltpu
from jax.sharding import PartitionSpec as P

LANES = 128
GELU_A = 0.7978845608028654
GELU_B = 0.7978845608028654 * 0.044715
HBM = pl.BlockSpec(memory_space=pltpu.HBM)
VMEM = pl.BlockSpec(memory_space=pltpu.VMEM)
MIB = 1024 * 1024


def call(kernel, name, outs, operands, hbm_in=0, hbm_out=0, scratch=(), limit=8, flops=0, moved=0):
    return pl.pallas_call(
        kernel,
        in_specs=[HBM] * hbm_in + [VMEM] * (len(operands) - hbm_in),
        out_specs=[HBM] * hbm_out + [VMEM] * (len(outs) - hbm_out),
        out_shape=outs,
        scratch_shapes=scratch,
        compiler_params=pltpu.CompilerParams(vmem_limit_bytes=limit * MIB),
        cost_estimate=pl.CostEstimate(flops=flops, bytes_accessed=moved, transcendentals=0),
        name=name,
    )(*operands)


def array(shape, dtype=jnp.float32):
    return jax.ShapeDtypeStruct(shape, dtype)


def limited(ahead, behind):
    return jnp.maximum(jnp.minimum(ahead, jnp.maximum(behind, 0.0)), jnp.minimum(behind, 0.0))


def face(speed):
    size = jnp.abs(speed)
    return speed > 0.0, speed, size * (0.5 - 0.5 * size)


def rows_after(q, faces):
    diffs = [b - a for a, b in zip(q[:-1], q[1:])]
    slopes = [None] + [limited(b, a) for a, b in zip(diffs[:-1], diffs[1:])]
    fluxes = []
    for j, (mask, speed, half) in enumerate(faces):
        edge = jnp.where(mask, q[j + 1], q[j + 2])
        slope = jnp.where(mask, slopes[j + 1], slopes[j + 2])
        fluxes.append(speed * edge + half * slope)
    return [q[j + 2] - (fluxes[j + 1] - fluxes[j]) for j in range(len(faces) - 1)]


def row_of(ref, start, count, rows):
    return ref[pl.ds(start, count, stride=rows), :]


def pack_kernel(parts, state_hbm, wind_hbm, kept_ref, winds_ref, up_ref, down_ref, sems):
    halves, fields, levels, rows, lanes = kept_ref.shape
    size = levels // parts
    wind_copies, copies = [], []
    for h in range(halves):
        lon = pl.ds(h * lanes, lanes)
        made = pltpu.make_async_copy(wind_hbm.at[:, :, lon], winds_ref.at[h], sems.at[h])
        wind_copies.append(made)
        for p in range(parts):
            some = pl.ds(p * size, size)
            made = pltpu.make_async_copy(
                state_hbm.at[:, some, :, lon], kept_ref.at[h, :, some], sems.at[halves + h * parts + p])
            made.start()
            copies.append((h, p, made))
        wind_copies[h].start()
    for h, p, made in copies:
        made.wait()
        here = slice(p * size, (p + 1) * size)
        flat = kept_ref.at[h].reshape(fields * levels * rows, lanes)
        for f in range(fields):
            base = (f * levels + p * size) * rows
            for r in range(2):
                first = row_of(flat, base + r, size, rows)
                down_ref[h, r * fields + f, here] = first.astype(jnp.bfloat16)
                last = row_of(flat, base + rows - 2 + r, size, rows)
                up_ref[h, r * fields + f, here] = last.astype(jnp.bfloat16)
    for h in range(halves):
        wind_copies[h].wait()
        speed = row_of(winds_ref.at[h].reshape(levels * rows, lanes), 0, levels, rows)
        high = speed.astype(jnp.bfloat16)
        down_ref[h, 2 * fields] = high
        down_ref[h, 2 * fields + 1] = (speed - high.astype(jnp.float32)).astype(jnp.bfloat16)


def pack(state, wind):
    fields, levels, rows, lons = state.shape
    halves = lons // LANES
    parts = 4
    return call(
        functools.partial(pack_kernel, parts), "pack",
        [
            array((halves, fields, levels, rows, LANES)),
            array((halves, levels, rows, LANES)),
            array((halves, 2 * fields, levels, LANES), jnp.bfloat16),
            array((halves, 2 * fields + 2, levels, LANES), jnp.bfloat16),
        ],
        (state, wind), hbm_in=2, scratch=[pltpu.SemaphoreType.DMA((halves * (parts + 1),))], moved=9_000_000)


def inner_kernel(kept_ref, winds_ref, out_ref):
    halves, fields, levels, rows, lanes = kept_ref.shape
    step = 8
    for h in range(halves):
        flat = kept_ref.at[h].reshape(fields * levels * rows, lanes)
        winds = winds_ref.at[h].reshape(levels * rows, lanes)

        @pl.loop(0, levels // step)
        def _(i):
            base = i * (step * rows)
            faces = [face(row_of(winds, base + r, step, rows)) for r in range(2, rows - 1)]
            level = pl.multiple_of(i * step, step)
            for f in range(fields):
                q = [row_of(flat, f * levels * rows + base + r, step, rows) for r in range(rows)]
                for r, value in enumerate(rows_after(q, faces)):
                    out_ref[h, r, f, pl.ds(level, step), :] = value


def inner(kept, winds):
    halves, fields, levels, rows, lanes = kept.shape
    return call(
        inner_kernel, "inner", [array((halves, rows - 4, fields, levels, lanes))], (kept, winds),
        flops=100_000_000, moved=8_000_000)[0]


def edge_kernel(kept_ref, winds_ref, above_ref, below_ref, out_ref, up_ref, down_ref):
    halves, fields, levels, rows, lanes = kept_ref.shape
    step = 16
    for h in range(halves):
        flat = kept_ref.at[h].reshape(fields * levels * rows, lanes)
        winds = winds_ref.at[h].reshape(levels * rows, lanes)

        @pl.loop(0, levels // step)
        def _(i):
            base = i * (step * rows)
            here = pl.ds(pl.multiple_of(i * step, step), step)
            wide = lambda ref, index: ref[h, index, here, :].astype(jnp.float32)
            speeds = {r: row_of(winds, base + r, step, rows) for r in (0, 1, 2, rows - 2, rows - 1)}
            speeds[rows] = wide(below_ref, 2 * fields) + wide(below_ref, 2 * fields + 1)
            for side, first in enumerate((0, rows - 2)):
                faces = [face(speeds[first + j]) for j in range(3)]
                for f in range(fields):
                    own = lambda r: row_of(flat, f * levels * rows + base + r, step, rows)
                    if side == 0:
                        q = [wide(above_ref, f), wide(above_ref, fields + f)] + [own(r) for r in range(4)]
                    else:
                        q = [own(r) for r in range(rows - 4, rows)] + [wide(below_ref, f), wide(below_ref, fields + f)]
                    sent = (down_ref, up_ref)[side]
                    for r, value in enumerate(rows_after(q, faces)):
                        out_ref[h, 2 * side + r, f, here, :] = value
                        sent[h, r * fields + f, here, :] = value.astype(jnp.bfloat16)


def edge(kept, winds, above, below):
    halves, fields, levels, rows, lanes = kept.shape
    sent = array((halves, 2 * fields, levels, lanes), jnp.bfloat16)
    return call(
        edge_kernel, "edge", [array((halves, 4, fields, levels, lanes)), sent, sent],
        (kept, winds, above, below), flops=100_000_000, moved=10_000_000)


def weights_kernel(first_ref, bias_ref, second_ref, remap_ref, first_out, second_out, split_out):
    inputs, hidden = first_ref.shape
    levels = remap_ref.shape[0]
    whole = remap_ref[...]
    r_high = whole.astype(jnp.bfloat16)
    r_low = (whole - r_high.astype(jnp.float32)).astype(jnp.bfloat16)
    for j in range(2):
        split_out[:levels, j * levels : (j + 1) * levels] = r_high
        split_out[levels:, j * levels : (j + 1) * levels] = r_low
    chunk = 256
    same = lambda d: lax.broadcasted_iota(jnp.int32, (chunk, chunk), d)
    unit = jnp.where(same(0) == same(1), 1.0, 0.0).astype(jnp.bfloat16)
    flip = lambda part: lax.dot_general(
        unit, part, (((1,), (1,)), ((), ())), preferred_element_type=jnp.float32).astype(jnp.bfloat16)
    small = unit[:LANES, :LANES]
    row = lax.broadcasted_iota(jnp.int32, (LANES, chunk), 0)
    for j in range(hidden // chunk):
        here = slice(j * chunk, (j + 1) * chunk)
        first_out[here, :inputs] = flip(first_ref[:, here])
        bias = bias_ref[:, here]
        high = bias.astype(jnp.bfloat16).astype(jnp.float32)
        middle = (bias - high).astype(jnp.bfloat16).astype(jnp.float32)
        low = bias - high - middle
        stacked = jnp.where(row == 0, high, jnp.where(row == 1, middle, jnp.where(row == 2, low, 0.0)))
        first_out[here, inputs:] = flip(stacked.astype(jnp.bfloat16))
        second_out[:, here] = lax.dot_general(
            small, second_ref[here, :], (((1,), (1,)), ((), ())),
            preferred_element_type=jnp.float32).astype(jnp.bfloat16)


def weights(w_first, bias, w_second, remap):
    inputs, hidden = w_first.shape
    levels = remap.shape[0]
    outputs = w_second.shape[1]
    return call(
        weights_kernel, "weights",
        [
            array((hidden, inputs + LANES), jnp.bfloat16),
            array((outputs, hidden), jnp.bfloat16),
            array((2 * levels, 2 * levels), jnp.bfloat16),
        ],
        (w_first, bias.reshape(1, hidden), w_second, remap), flops=100_000_000, moved=7_000_000)


def network(x, w1_ref, w2_ref):
    hidden = w1_ref.shape[0]
    chunk = 256
    total = None
    for c in range(hidden // chunk):
        v = jnp.dot(w1_ref[c * chunk : (c + 1) * chunk, :], x, preferred_element_type=jnp.float32)
        h = 0.5 * v
        t = jnp.tanh(v * (GELU_A + GELU_B * (v * v)))
        g = (h + h * t).astype(jnp.bfloat16)
        part = jnp.dot(w2_ref[:, c * chunk : (c + 1) * chunk], g, preferred_element_type=jnp.float32)
        total = part if total is None else total + part
    return total


def finish_kernel(edges, *refs):
    if edges:
        (mid, edg, wnd, scale, rcat, w1, w2, above, below, last, done, out_hbm, a, x, rem, out, sems) = refs
    else:
        (mid, edg, wnd, scale, rcat, w1, w2, out, a, x, rem) = refs
    halves, _, fields, levels, lanes = mid.shape
    rows = wnd.shape[2]
    inputs = fields * levels
    row = lax.broadcasted_iota(jnp.int32, (x.shape[1] - inputs, x.shape[2]), 0)
    for u in range(2):
        x[u, inputs:, :] = jnp.where(row < 3, 1.0, 0.0).astype(jnp.bfloat16)

    step = 16
    stores = []
    for h in range(halves):
        winds = wnd.at[h].reshape(levels * rows, lanes)

        @pl.loop(0, levels // step)
        def _(i):
            here = pl.ds(pl.multiple_of(i * step, step), step)
            there = pl.ds(pl.multiple_of(levels + i * step, step), step)
            base = i * (step * rows)
            wide = lambda ref, index: ref[h, index, here, :].astype(jnp.float32)
            if edges:
                needed = (0, 1, 2, rows - 2, rows - 1)
                speeds = {r: row_of(winds, base + r, step, rows) for r in needed}
                speeds[rows] = wide(last, 2 * fields) + wide(last, 2 * fields + 1)
                groups = ((0, 2), (rows - 2, 2))
            else:
                speeds = {r: row_of(winds, base + r, step, rows) for r in range(2, rows - 1)}
                groups = ((2, 4),)
            for first, many in groups:
                faces = [face(speeds[first + j]) for j in range(many + 1)]
                for f in range(fields):
                    kept = lambda r: (mid[h, r - 2, f, here, :] if 2 <= r < rows - 2 else
                                      edg[h, r if r < 2 else r - rows + 4, f, here, :])
                    q = []
                    for r in range(first - 2, first + many + 2):
                        if r < 0:
                            q.append(wide(above, (r + 2) * fields + f))
                        elif r >= rows:
                            q.append(wide(below, (r - rows) * fields + f))
                        else:
                            q.append(kept(r))
                    for j, value in enumerate(rows_after(q, faces)):
                        if edges:
                            u, place = (0 if first == 0 else 1), j
                        else:
                            u, place = j // 2, j % 2
                        cols = pl.ds(place * lanes, lanes)
                        high = value.astype(jnp.bfloat16)
                        a[u, f, here, cols] = high
                        a[u, f, there, cols] = (value - high.astype(jnp.float32)).astype(jnp.bfloat16)

        starts = (0, rows - 2) if edges else (2, 4)
        if edges:
            flat = out.at[h].reshape(fields * levels * rows, lanes)

        def put(f, u, place, value):
            if edges:
                flat[pl.ds(f * levels * rows + starts[u] + place, levels, stride=rows), :] = value
            else:
                out[h, 2 * u + place, f] = value

        if edges:
            for f in range(fields):
                for r in range(2, rows - 2):
                    flat[pl.ds(f * levels * rows + r, levels, stride=rows), :] = done[h, r - 2, f]
        for u in range(2):
            for f in range(fields):
                both = jnp.dot(rcat[...], a[u, f], preferred_element_type=jnp.float32)
                value = both[:levels] + both[levels:]
                x[u, f * levels : (f + 1) * levels, :] = value.astype(jnp.bfloat16)
                if f == 0:
                    rem[u] = value
                else:
                    for place in range(2):
                        put(f, u, place, value[:, place * lanes : (place + 1) * lanes])
        if edges:
            lon = pl.ds(h * lanes, lanes)
            made = pltpu.make_async_copy(
                out.at[h, pl.ds(1, fields - 1)], out_hbm.at[pl.ds(1, fields - 1), :, :, lon], sems.at[2 * h])
            made.start()
            stores.append(made)
        for u in range(2):
            net = network(x[u], w1, w2)
            for place in range(2):
                r = starts[u] + place
                part = slice(place * lanes, (place + 1) * lanes)
                light = scale[r : r + 1, h * lanes : (h + 1) * lanes]
                put(0, u, place, rem[u, :, part] + net[:, part] * light)
        if edges:
            made = pltpu.make_async_copy(out.at[h, 0], out_hbm.at[0, :, :, lon], sems.at[2 * h + 1])
            made.start()
            stores.append(made)
    for made in stores:
        made.wait()


def finish(edges, mid, edge_rows, wind, scale, rcat, w1, w2, *more):
    halves, inner_rows, fields, levels, lanes = mid.shape
    rows = inner_rows + 4
    scratch = [
        pltpu.VMEM((2, fields, 2 * levels, 2 * lanes), jnp.bfloat16),
        pltpu.VMEM((2, w1.shape[1], 2 * lanes), jnp.bfloat16),
        pltpu.VMEM((2, levels, 2 * lanes), jnp.float32),
    ]
    if edges:
        scratch += [
            pltpu.VMEM((halves, fields, levels, rows, lanes), jnp.float32),
            pltpu.SemaphoreType.DMA((2 * halves,)),
        ]
        outs = [array((fields, levels, rows, halves * lanes))]
    else:
        outs = [array(mid.shape)]
    return call(
        functools.partial(finish_kernel, edges), "finish_edges" if edges else "finish_inner", outs,
        (mid, edge_rows, wind, scale, rcat, w1, w2) + more, hbm_out=1 if edges else 0, scratch=scratch,
        limit=16, flops=4_000_000_000, moved=12_000_000)[0]


def shards(state, wind, sunlight, day_list, w_first, bias, w_second, remap):
    fields, levels, rows, lons = state.shape
    halves = lons // LANES
    count = lax.axis_size("lat")
    forward = [(i, i + 1) for i in range(count - 1)]
    back = [(i + 1, i) for i in range(count - 1)]
    kept, winds, up, down = pack(state, wind)
    above = lax.ppermute(up, "lat", forward)
    below = lax.ppermute(down, "lat", back)

    mid = inner(kept, winds)
    w1, w2, rcat = weights(w_first, bias, w_second, remap)
    blocks = day_list.shape[1]
    lit = jnp.any(day_list[0][None, :] == jnp.arange(blocks, dtype=jnp.int32)[:, None], axis=1)
    lit = jnp.broadcast_to(lit.astype(jnp.float32).reshape(rows, halves, 1), (rows, halves, LANES))
    scale = sunlight * lit.reshape(rows, lons)

    kept, mid, w1, w2, rcat, scale = lax.optimization_barrier((kept, mid, w1, w2, rcat, scale))
    edge_rows, up2, down2 = edge(kept, winds, above, below)
    above2 = lax.ppermute(up2, "lat", forward)
    below2 = lax.ppermute(down2, "lat", back)
    partial = finish(False, mid, edge_rows, winds, scale, rcat, w1, w2)
    return finish(True, mid, edge_rows, winds, scale, rcat, w1, w2, above2, below2, below, partial)


def solution(mesh):
    placed = (
        P("member", None, "lat", None),
        P("member", "lat", None),
        P(("member", "lat"), None),
        P(("member", "lat"), None),
        P(),
        P(),
        P(),
        P(),
    )
    return jax.shard_map(
        shards,
        mesh=mesh,
        in_specs=placed,
        out_specs=P("member", None, "lat", None),
        check_vma=False,
    )
```

```python
import functools
import jax
import jax.numpy as jnp
from jax import lax
from jax.experimental import pallas as pl
from jax.experimental.pallas import tpu as pltpu
from jax.sharding import PartitionSpec as P

LANES = 128
GELU_A = 0.7978845608028654
GELU_B = 0.7978845608028654 * 0.044715
HBM = pl.BlockSpec(memory_space=pltpu.HBM)
VMEM = pl.BlockSpec(memory_space=pltpu.VMEM)
MIB = 1024 * 1024


def call(kernel, name, outs, operands, ins=None, out_specs=None, scratch=(), limit=8, flops=0, moved=0, alias=None):
    return pl.pallas_call(
        kernel,
        in_specs=ins or [VMEM] * len(operands),
        out_specs=out_specs or [VMEM] * len(outs),
        out_shape=outs,
        scratch_shapes=scratch,
        input_output_aliases=alias or {},
        compiler_params=pltpu.CompilerParams(vmem_limit_bytes=limit * MIB),
        cost_estimate=pl.CostEstimate(flops=flops, bytes_accessed=moved, transcendentals=0),
        name=name,
    )(*operands)


def array(shape, dtype=jnp.float32):
    return jax.ShapeDtypeStruct(shape, dtype)


def limited(ahead, behind):
    return jnp.maximum(jnp.minimum(ahead, jnp.maximum(behind, 0.0)), jnp.minimum(behind, 0.0))


def face(speed):
    size = jnp.abs(speed)
    return speed > 0.0, speed, size * (0.5 - 0.5 * size)


def rows_after(q, faces):
    diffs = [b - a for a, b in zip(q[:-1], q[1:])]
    slopes = [None] + [limited(b, a) for a, b in zip(diffs[:-1], diffs[1:])]
    fluxes = []
    for j, (mask, speed, half) in enumerate(faces):
        edge = jnp.where(mask, q[j + 1], q[j + 2])
        slope = jnp.where(mask, slopes[j + 1], slopes[j + 2])
        fluxes.append(speed * edge + half * slope)
    return [q[j + 2] - (fluxes[j + 1] - fluxes[j]) for j in range(len(faces) - 1)]


def row_of(ref, start, count, rows):
    return ref[pl.ds(start, count, stride=rows), :]


def pack_kernel(half, parts, state_hbm, wind_hbm, kept_ref, winds_ref, up_ref, down_ref, sems):
    fields, levels, rows, lanes = kept_ref.shape
    size = levels // parts
    lon = pl.ds(half * lanes, lanes)
    copies = []
    for p in range(parts):
        some = pl.ds(p * size, size)
        made = pltpu.make_async_copy(state_hbm.at[:, some, :, lon], kept_ref.at[:, some], sems.at[p])
        made.start()
        copies.append(made)
    winds = pltpu.make_async_copy(wind_hbm.at[:, :, lon], winds_ref, sems.at[parts])
    winds.start()
    flat = kept_ref.reshape(fields * levels * rows, lanes)
    for p, made in enumerate(copies):
        made.wait()
        here = slice(p * size, (p + 1) * size)
        for f in range(fields):
            base = (f * levels + p * size) * rows
            for r in range(2):
                first = row_of(flat, base + r, size, rows)
                down_ref[r * fields + f, here] = first.astype(jnp.bfloat16)
                last = row_of(flat, base + rows - 2 + r, size, rows)
                up_ref[r * fields + f, here] = last.astype(jnp.bfloat16)
    winds.wait()
    speed = row_of(winds_ref.reshape(levels * rows, lanes), 0, levels, rows)
    high = speed.astype(jnp.bfloat16)
    down_ref[2 * fields] = high
    down_ref[2 * fields + 1] = (speed - high.astype(jnp.float32)).astype(jnp.bfloat16)


def pack(half, state, wind):
    fields, levels, rows, lons = state.shape
    parts = 4
    return call(
        functools.partial(pack_kernel, half, parts), f"pack{half}",
        [
            array((fields, levels, rows, LANES)),
            array((levels, rows, LANES)),
            array((2 * fields, levels, LANES), jnp.bfloat16),
            array((2 * fields + 2, levels, LANES), jnp.bfloat16),
        ],
        (state, wind), ins=[HBM, HBM], scratch=[pltpu.SemaphoreType.DMA((parts + 1,))], moved=5_000_000)


def inner_kernel(kept_ref, winds_ref, out_ref):
    fields, levels, rows, lanes = kept_ref.shape
    step = 8
    flat = kept_ref.reshape(fields * levels * rows, lanes)
    winds = winds_ref.reshape(levels * rows, lanes)

    @pl.loop(0, levels // step)
    def _(i):
        base = i * (step * rows)
        faces = [face(row_of(winds, base + r, step, rows)) for r in range(2, rows - 1)]
        level = pl.multiple_of(i * step, step)
        for f in range(fields):
            q = [row_of(flat, f * levels * rows + base + r, step, rows) for r in range(rows)]
            for r, value in enumerate(rows_after(q, faces)):
                out_ref[r, f, pl.ds(level, step), :] = value


def inner(half, kept, winds):
    fields, levels, rows, lanes = kept.shape
    return call(
        inner_kernel, f"inner{half}", [array((rows - 4, fields, levels, lanes))], (kept, winds),
        flops=50_000_000, moved=4_000_000)[0]


def edge_kernel(kept_ref, winds_ref, above_ref, below_ref, out_ref, up_ref, down_ref):
    fields, levels, rows, lanes = kept_ref.shape
    step = 16
    flat = kept_ref.reshape(fields * levels * rows, lanes)
    winds = winds_ref.reshape(levels * rows, lanes)

    @pl.loop(0, levels // step)
    def _(i):
        base = i * (step * rows)
        here = pl.ds(pl.multiple_of(i * step, step), step)
        wide = lambda ref, index: ref[index, here, :].astype(jnp.float32)
        speeds = {r: row_of(winds, base + r, step, rows) for r in (0, 1, 2, rows - 2, rows - 1)}
        speeds[rows] = wide(below_ref, 2 * fields) + wide(below_ref, 2 * fields + 1)
        for side, first in enumerate((0, rows - 2)):
            faces = [face(speeds[first + j]) for j in range(3)]
            for f in range(fields):
                own = lambda r: row_of(flat, f * levels * rows + base + r, step, rows)
                if side == 0:
                    q = [wide(above_ref, f), wide(above_ref, fields + f)] + [own(r) for r in range(4)]
                else:
                    q = [own(r) for r in range(rows - 4, rows)] + [wide(below_ref, f), wide(below_ref, fields + f)]
                sent = (down_ref, up_ref)[side]
                for r, value in enumerate(rows_after(q, faces)):
                    out_ref[2 * side + r, f, here, :] = value
                    sent[r * fields + f, here, :] = value.astype(jnp.bfloat16)


def edge(half, kept, winds, above, below):
    fields, levels, rows, lanes = kept.shape
    sent = array((2 * fields, levels, lanes), jnp.bfloat16)
    return call(
        edge_kernel, f"edge{half}", [array((4, fields, levels, lanes)), sent, sent],
        (kept, winds, above, below), flops=50_000_000, moved=5_000_000)


def weights_kernel(first_ref, bias_ref, second_ref, remap_ref, first_out, second_out, split_out):
    inputs, hidden = first_ref.shape
    levels = remap_ref.shape[0]
    whole = remap_ref[...]
    r_high = whole.astype(jnp.bfloat16)
    r_low = (whole - r_high.astype(jnp.float32)).astype(jnp.bfloat16)
    for j in range(2):
        split_out[:levels, j * levels : (j + 1) * levels] = r_high
        split_out[levels:, j * levels : (j + 1) * levels] = r_low
    chunk = 256
    same = lambda d: lax.broadcasted_iota(jnp.int32, (chunk, chunk), d)
    unit = jnp.where(same(0) == same(1), 1.0, 0.0).astype(jnp.bfloat16)
    flip = lambda part: lax.dot_general(
        unit, part, (((1,), (1,)), ((), ())), preferred_element_type=jnp.float32).astype(jnp.bfloat16)
    small = unit[:LANES, :LANES]
    row = lax.broadcasted_iota(jnp.int32, (LANES, chunk), 0)
    for j in range(hidden // chunk):
        here = slice(j * chunk, (j + 1) * chunk)
        first_out[here, :inputs] = flip(first_ref[:, here])
        bias = bias_ref[:, here]
        high = bias.astype(jnp.bfloat16).astype(jnp.float32)
        middle = (bias - high).astype(jnp.bfloat16).astype(jnp.float32)
        low = bias - high - middle
        stacked = jnp.where(row == 0, high, jnp.where(row == 1, middle, jnp.where(row == 2, low, 0.0)))
        first_out[here, inputs:] = flip(stacked.astype(jnp.bfloat16))
        second_out[:, here] = lax.dot_general(
            small, second_ref[here, :], (((1,), (1,)), ((), ())),
            preferred_element_type=jnp.float32).astype(jnp.bfloat16)


def weights(w_first, bias, w_second, remap):
    inputs, hidden = w_first.shape
    levels = remap.shape[0]
    outputs = w_second.shape[1]
    return call(
        weights_kernel, "weights",
        [
            array((hidden, inputs + LANES), jnp.bfloat16),
            array((outputs, hidden), jnp.bfloat16),
            array((2 * levels, 2 * levels), jnp.bfloat16),
        ],
        (w_first, bias.reshape(1, hidden), w_second, remap), flops=50_000_000, moved=7_000_000)


def network(x, w1_ref, w2_ref, g_ref):
    hidden = w1_ref.shape[0]
    chunk = 512
    for c in range(hidden // chunk):
        here = slice(c * chunk, (c + 1) * chunk)
        v = jnp.dot(w1_ref[here, :], x, preferred_element_type=jnp.float32)
        h = 0.5 * v
        t = jnp.tanh(v * (GELU_A + GELU_B * (v * v)))
        g_ref[here, :] = (h + h * t).astype(jnp.bfloat16)
    return jnp.dot(w2_ref[...], g_ref[...], preferred_element_type=jnp.float32)


def finish_kernel(edges, half, halves, *refs):
    if edges:
        (days, mid, edg, wnd, sun, rcat, w1, w2, above, below, last, _, *refs) = refs
        (out_hbm, out, a, x, rem, g, sems) = refs[-7:]
    else:
        (days, mid, edg, wnd, sun, rcat, w1, w2, out, a, x, rem, g) = refs
    _, fields, levels, lanes = mid.shape
    rows = wnd.shape[1]
    inputs = fields * levels
    row = lax.broadcasted_iota(jnp.int32, (x.shape[1] - inputs, x.shape[2]), 0)
    for u in range(2):
        x[u, inputs:, :] = jnp.where(row < 3, 1.0, 0.0).astype(jnp.bfloat16)

    step = 16
    winds = wnd.reshape(levels * rows, lanes)

    @pl.loop(0, levels // step)
    def _(i):
        here = pl.ds(pl.multiple_of(i * step, step), step)
        there = pl.ds(pl.multiple_of(levels + i * step, step), step)
        base = i * (step * rows)
        wide = lambda ref, index: ref[index, here, :].astype(jnp.float32)
        if edges:
            needed = (0, 1, 2, rows - 2, rows - 1)
            speeds = {r: row_of(winds, base + r, step, rows) for r in needed}
            speeds[rows] = wide(last, 2 * fields) + wide(last, 2 * fields + 1)
            groups = ((0, 2), (rows - 2, 2))
        else:
            speeds = {r: row_of(winds, base + r, step, rows) for r in range(2, rows - 1)}
            groups = ((2, 4),)
        for first, many in groups:
            faces = [face(speeds[first + j]) for j in range(many + 1)]
            for f in range(fields):
                kept = lambda r: (mid[r - 2, f, here, :] if 2 <= r < rows - 2 else
                                  edg[r if r < 2 else r - rows + 4, f, here, :])
                q = []
                for r in range(first - 2, first + many + 2):
                    if r < 0:
                        q.append(wide(above, (r + 2) * fields + f))
                    elif r >= rows:
                        q.append(wide(below, (r - rows) * fields + f))
                    else:
                        q.append(kept(r))
                for j, value in enumerate(rows_after(q, faces)):
                    if edges:
                        u, place = (0 if first == 0 else 1), j
                    else:
                        u, place = j // 2, j % 2
                    cols = pl.ds(place * lanes, lanes)
                    high = value.astype(jnp.bfloat16)
                    a[u, f, here, cols] = high
                    a[u, f, there, cols] = (value - high.astype(jnp.float32)).astype(jnp.bfloat16)

    starts = (0, rows - 2) if edges else (2, 4)
    flat = out.reshape(fields * levels * rows, lanes)

    def put(f, u, place, value):
        flat[pl.ds(f * levels * rows + starts[u] + place, levels, stride=rows), :] = value

    for u in range(2):
        for f in range(fields):
            both = jnp.dot(rcat[...], a[u, f], preferred_element_type=jnp.float32)
            value = both[:levels] + both[levels:]
            x[u, f * levels : (f + 1) * levels, :] = value.astype(jnp.bfloat16)
            if f == 0:
                rem[u] = value
            else:
                for place in range(2):
                    put(f, u, place, value[:, place * lanes : (place + 1) * lanes])
    stores = []
    lon = pl.ds(half * lanes, lanes)
    if edges:
        most = pl.ds(1, fields - 1)
        made = pltpu.make_async_copy(out.at[most], out_hbm.at[most, :, :, lon], sems.at[0])
        made.start()
        stores.append(made)
    for u in range(2):
        net = network(x[u], w1, w2, g.at[u])
        for place in range(2):
            r = starts[u] + place
            lit = days[0, 0] == r * halves + half
            for i in range(1, days.shape[1]):
                lit = jnp.logical_or(lit, days[0, i] == r * halves + half)
            part = slice(place * lanes, (place + 1) * lanes)
            light = sun[r : r + 1, half * lanes : (half + 1) * lanes] * jnp.where(lit, 1.0, 0.0)
            put(0, u, place, rem[u, :, part] + net[:, part] * light)
    if edges:
        made = pltpu.make_async_copy(out.at[0], out_hbm.at[0, :, :, lon], sems.at[1])
        made.start()
        stores.append(made)
    for made in stores:
        made.wait()


def finish(edges, half, halves, days, mid, edge_rows, wind, sun, rcat, w1, w2, *more):
    _, fields, levels, lanes = mid.shape
    rows = wind.shape[1]
    scratch = [
        pltpu.VMEM((2, fields, 2 * levels, 2 * lanes), jnp.bfloat16),
        pltpu.VMEM((2, w1.shape[1], 2 * lanes), jnp.bfloat16),
        pltpu.VMEM((2, levels, 2 * lanes), jnp.float32),
        pltpu.VMEM((2, w1.shape[0], 2 * lanes), jnp.bfloat16),
    ]
    operands = (days, mid, edge_rows, wind, sun, rcat, w1, w2) + more
    ins = [pl.BlockSpec(memory_space=pltpu.SMEM)] + [VMEM] * (len(operands) - 1)
    outs = [array((fields, levels, rows, lanes))]
    out_specs = [VMEM]
    alias = {}
    if edges:
        scratch.append(pltpu.SemaphoreType.DMA((2,)))
        outs = [array((fields, levels, rows, halves * lanes))] + outs
        out_specs = [HBM, VMEM]
        alias = {11: 1}
        if len(operands) > 12:
            ins[12] = HBM
            alias[12] = 0
    return call(
        functools.partial(finish_kernel, edges, half, halves), f"finish_{'edges' if edges else 'inner'}{half}", outs,
        operands, ins=ins, out_specs=out_specs, scratch=scratch, alias=alias,
        limit=16, flops=2_000_000_000, moved=6_000_000)[0]


def shards(state, wind, sunlight, day_list, w_first, bias, w_second, remap):
    halves = state.shape[3] // LANES
    count = lax.axis_size("lat")
    forward = [(i, i + 1) for i in range(count - 1)]
    back = [(i + 1, i) for i in range(count - 1)]
    every = range(halves)
    state = pltpu.with_memory_space_constraint(state, pltpu.HBM)
    wind = pltpu.with_memory_space_constraint(wind, pltpu.HBM)
    kept, winds, above, below, mid = [], [], [], [], []
    for h in every:
        k, w, up, down = pack(h, state, wind)
        kept.append(k)
        winds.append(w)
        above.append(lax.ppermute(up, "lat", forward))
        below.append(lax.ppermute(down, "lat", back))
    for h in every:
        mid.append(inner(h, kept[h], winds[h]))
    w1, w2, rcat = weights(w_first, bias, w_second, remap)
    mid, w1, w2, rcat, above[0], below[0] = lax.optimization_barrier((mid, w1, w2, rcat, above[0], below[0]))
    edges, above2, below2, partial = [], [], [], []
    for h in every:
        rows, up, down = edge(h, kept[h], winds[h], above[h], below[h])
        edges.append(rows)
        above2.append(lax.ppermute(up, "lat", forward))
        below2.append(lax.ppermute(down, "lat", back))
        partial.append(finish(False, h, halves, day_list, mid[h], rows, winds[h], sunlight, rcat, w1, w2))
        if h + 1 < halves:
            above[h + 1], below[h + 1], partial[h] = lax.optimization_barrier((above[h + 1], below[h + 1], partial[h]))
    above2[0], below2[0], partial = lax.optimization_barrier((above2[0], below2[0], partial))
    out = ()
    for h in every:
        more = (above2[h], below2[h], below[h], partial[h]) + out
        out = (finish(True, h, halves, day_list, mid[h], edges[h], winds[h], sunlight, rcat, w1, w2, *more),)
        if h + 1 < halves:
            above2[h + 1], below2[h + 1], out = lax.optimization_barrier((above2[h + 1], below2[h + 1], out))
    return out[0]


def solution(mesh):
    placed = (
        P("member", None, "lat", None),
        P("member", "lat", None),
        P(("member", "lat"), None),
        P(("member", "lat"), None),
        P(),
        P(),
        P(),
        P(),
    )
    return jax.shard_map(
        shards,
        mesh=mesh,
        in_specs=placed,
        out_specs=P("member", None, "lat", None),
        check_vma=False,
    )
```

```python
import functools
import jax
import jax.numpy as jnp
from jax import lax
from jax.experimental import pallas as pl
from jax.experimental.pallas import tpu as pltpu
from jax.sharding import PartitionSpec as P

LANES = 128
GELU_A = 0.7978845608028654
GELU_B = 0.7978845608028654 * 0.044715
HBM = pl.BlockSpec(memory_space=pltpu.HBM)
VMEM = pl.BlockSpec(memory_space=pltpu.VMEM)
MIB = 1024 * 1024


def call(kernel, name, outs, operands, ins=None, out_specs=None, scratch=(), limit=8, flops=0, moved=0, alias=None):
    return pl.pallas_call(
        kernel,
        in_specs=ins or [VMEM] * len(operands),
        out_specs=out_specs or [VMEM] * len(outs),
        out_shape=outs,
        scratch_shapes=scratch,
        input_output_aliases=alias or {},
        compiler_params=pltpu.CompilerParams(vmem_limit_bytes=limit * MIB),
        cost_estimate=pl.CostEstimate(flops=flops, bytes_accessed=moved, transcendentals=0),
        name=name,
    )(*operands)


def array(shape, dtype=jnp.float32):
    return jax.ShapeDtypeStruct(shape, dtype)


def limited(ahead, behind):
    return jnp.maximum(jnp.minimum(ahead, jnp.maximum(behind, 0.0)), jnp.minimum(behind, 0.0))


def face(speed):
    size = jnp.abs(speed)
    return speed > 0.0, speed, size * (0.5 - 0.5 * size)


def rows_after(q, faces):
    diffs = [b - a for a, b in zip(q[:-1], q[1:])]
    slopes = [None] + [limited(b, a) for a, b in zip(diffs[:-1], diffs[1:])]
    fluxes = []
    for j, (mask, speed, half) in enumerate(faces):
        edge = jnp.where(mask, q[j + 1], q[j + 2])
        slope = jnp.where(mask, slopes[j + 1], slopes[j + 2])
        fluxes.append(speed * edge + half * slope)
    return [q[j + 2] - (fluxes[j + 1] - fluxes[j]) for j in range(len(faces) - 1)]


def is_even():
    return lax.rem(lax.axis_index("lat"), 2) == 0


def by_parity(body, near, far):
    pl.when(is_even())(lambda: body(far, near))
    pl.when(jnp.logical_not(is_even()))(lambda: body(near, far))


def row_of(ref, start, count, rows):
    return ref[pl.ds(start, count, stride=rows), :]


def pack_kernel(half, parts, state_hbm, wind_hbm, kept_ref, winds_ref, near_ref, far_ref, sems):
    fields, levels, rows, lanes = kept_ref.shape
    size = levels // parts
    lon = pl.ds(half * lanes, lanes)
    copies = []
    for p in range(parts):
        some = pl.ds(p * size, size)
        made = pltpu.make_async_copy(state_hbm.at[:, some, :, lon], kept_ref.at[:, some], sems.at[p])
        made.start()
        copies.append(made)
    winds = pltpu.make_async_copy(wind_hbm.at[:, :, lon], winds_ref, sems.at[parts])
    winds.start()
    flat = kept_ref.reshape(fields * levels * rows, lanes)
    even = is_even()
    for p, made in enumerate(copies):
        made.wait()
        here = slice(p * size, (p + 1) * size)
        for f in range(fields):
            base = (f * levels + p * size) * rows
            for r in range(2):
                for ref, start in ((near_ref, jnp.where(even, rows - 2, 0)), (far_ref, jnp.where(even, 0, rows - 2))):
                    value = row_of(flat, base + start + r, size, rows)
                    ref[r * fields + f, here] = value.astype(jnp.bfloat16)
    winds.wait()
    speed = row_of(winds_ref.reshape(levels * rows, lanes), 0, levels, rows)
    high = speed.astype(jnp.bfloat16)
    low = (speed - high.astype(jnp.float32)).astype(jnp.bfloat16)
    for ref in (near_ref, far_ref):
        ref[2 * fields] = high
        ref[2 * fields + 1] = low


def pack(half, state, wind):
    fields, levels, rows, lons = state.shape
    parts = 4
    return call(
        functools.partial(pack_kernel, half, parts), f"pack{half}",
        [
            array((fields, levels, rows, LANES)),
            array((levels, rows, LANES)),
            array((2 * fields + 2, levels, LANES), jnp.bfloat16),
            array((2 * fields + 2, levels, LANES), jnp.bfloat16),
        ],
        (state, wind), ins=[HBM, HBM], scratch=[pltpu.SemaphoreType.DMA((parts + 1,))], moved=5_000_000)


def inner_kernel(kept_ref, winds_ref, out_ref):
    fields, levels, rows, lanes = kept_ref.shape
    step = 8
    flat = kept_ref.reshape(fields * levels * rows, lanes)
    winds = winds_ref.reshape(levels * rows, lanes)

    @pl.loop(0, levels // step)
    def _(i):
        base = i * (step * rows)
        faces = [face(row_of(winds, base + r, step, rows)) for r in range(2, rows - 1)]
        level = pl.multiple_of(i * step, step)
        for f in range(fields):
            q = [row_of(flat, f * levels * rows + base + r, step, rows) for r in range(rows)]
            for r, value in enumerate(rows_after(q, faces)):
                out_ref[r, f, pl.ds(level, step), :] = value


def inner(half, kept, winds):
    fields, levels, rows, lanes = kept.shape
    return call(
        inner_kernel, f"inner{half}", [array((rows - 4, fields, levels, lanes))], (kept, winds),
        flops=50_000_000, moved=4_000_000)[0]


def edge_kernel(kept_ref, winds_ref, near_in, far_in, out_ref, near_out, far_out):
    fields, levels, rows, lanes = kept_ref.shape
    step = 16
    flat = kept_ref.reshape(fields * levels * rows, lanes)
    winds = winds_ref.reshape(levels * rows, lanes)

    def body(top, bottom):
        above_ref, down_ref = top
        below_ref, up_ref = bottom

        @pl.loop(0, levels // step)
        def _(i):
            base = i * (step * rows)
            here = pl.ds(pl.multiple_of(i * step, step), step)
            wide = lambda ref, index: ref[index, here, :].astype(jnp.float32)
            speeds = {r: row_of(winds, base + r, step, rows) for r in (0, 1, 2, rows - 2, rows - 1)}
            speeds[rows] = wide(below_ref, 2 * fields) + wide(below_ref, 2 * fields + 1)
            for side, first in enumerate((0, rows - 2)):
                faces = [face(speeds[first + j]) for j in range(3)]
                for f in range(fields):
                    own = lambda r: row_of(flat, f * levels * rows + base + r, step, rows)
                    if side == 0:
                        q = [wide(above_ref, f), wide(above_ref, fields + f)] + [own(r) for r in range(4)]
                    else:
                        q = [own(r) for r in range(rows - 4, rows)] + [wide(below_ref, f), wide(below_ref, fields + f)]
                    sent = (down_ref, up_ref)[side]
                    for r, value in enumerate(rows_after(q, faces)):
                        out_ref[2 * side + r, f, here, :] = value
                        sent[r * fields + f, here, :] = value.astype(jnp.bfloat16)

    by_parity(body, (near_in, near_out), (far_in, far_out))


def edge(half, kept, winds, near, far):
    fields, levels, rows, lanes = kept.shape
    sent = array((2 * fields, levels, lanes), jnp.bfloat16)
    return call(
        edge_kernel, f"edge{half}", [array((4, fields, levels, lanes)), sent, sent],
        (kept, winds, near, far), flops=50_000_000, moved=5_000_000)


def weights_kernel(first_ref, bias_ref, second_ref, remap_ref, first_out, second_out, split_out):
    inputs, hidden = first_ref.shape
    levels = remap_ref.shape[0]
    whole = remap_ref[...]
    r_high = whole.astype(jnp.bfloat16)
    r_low = (whole - r_high.astype(jnp.float32)).astype(jnp.bfloat16)
    for j in range(2):
        split_out[:levels, j * levels : (j + 1) * levels] = r_high
        split_out[levels:, j * levels : (j + 1) * levels] = r_low
    chunk = 256
    same = lambda d: lax.broadcasted_iota(jnp.int32, (chunk, chunk), d)
    unit = jnp.where(same(0) == same(1), 1.0, 0.0).astype(jnp.bfloat16)
    flip = lambda part: lax.dot_general(
        unit, part, (((1,), (1,)), ((), ())), preferred_element_type=jnp.float32).astype(jnp.bfloat16)
    small = unit[:LANES, :LANES]
    row = lax.broadcasted_iota(jnp.int32, (LANES, chunk), 0)
    for j in range(hidden // chunk):
        here = slice(j * chunk, (j + 1) * chunk)
        first_out[here, :inputs] = flip(first_ref[:, here])
        bias = bias_ref[:, here]
        high = bias.astype(jnp.bfloat16).astype(jnp.float32)
        middle = (bias - high).astype(jnp.bfloat16).astype(jnp.float32)
        low = bias - high - middle
        stacked = jnp.where(row == 0, high, jnp.where(row == 1, middle, jnp.where(row == 2, low, 0.0)))
        first_out[here, inputs:] = flip(stacked.astype(jnp.bfloat16))
        second_out[:, here] = lax.dot_general(
            small, second_ref[here, :], (((1,), (1,)), ((), ())),
            preferred_element_type=jnp.float32).astype(jnp.bfloat16)


def weights(w_first, bias, w_second, remap):
    inputs, hidden = w_first.shape
    levels = remap.shape[0]
    outputs = w_second.shape[1]
    return call(
        weights_kernel, "weights",
        [
            array((hidden, inputs + LANES), jnp.bfloat16),
            array((outputs, hidden), jnp.bfloat16),
            array((2 * levels, 2 * levels), jnp.bfloat16),
        ],
        (w_first, bias.reshape(1, hidden), w_second, remap), flops=50_000_000, moved=7_000_000)


def network(x, w1_ref, w2_ref, g_ref):
    hidden = w1_ref.shape[0]
    chunk = 512
    for c in range(hidden // chunk):
        here = slice(c * chunk, (c + 1) * chunk)
        v = jnp.dot(w1_ref[here, :], x, preferred_element_type=jnp.float32)
        h = 0.5 * v
        t = jnp.tanh(v * (GELU_A + GELU_B * (v * v)))
        g_ref[here, :] = (h + h * t).astype(jnp.bfloat16)
    return jnp.dot(w2_ref[...], g_ref[...], preferred_element_type=jnp.float32)


def finish_kernel(edges, half, halves, *refs):
    last_half = edges and half == halves - 1
    if last_half:
        (days, mid, edg, wnd, sun, rcat, w1, w2, near2, far2, near1, far1, _, *refs) = refs
        *ready, out_hbm, out, a, x, rem, g, sems = refs
    elif edges:
        (days, mid, edg, wnd, sun, rcat, w1, w2, near2, far2, near1, far1, _, out, a, x, rem, g) = refs
    else:
        (days, mid, edg, wnd, sun, rcat, w1, w2, out, a, x, rem, g) = refs
    _, fields, levels, lanes = mid.shape
    rows = wnd.shape[1]
    inputs = fields * levels
    most = pl.ds(1, fields - 1)
    stores = []

    def store(source, target):
        made = pltpu.make_async_copy(source, target, sems.at[len(stores)])
        made.start()
        stores.append(made)

    if last_half:
        for h, source in enumerate(ready):
            store(source, out_hbm.at[:, :, :, pl.ds(h * lanes, lanes)])
    row = lax.broadcasted_iota(jnp.int32, (x.shape[1] - inputs, x.shape[2]), 0)
    for u in range(2):
        x[u, inputs:, :] = jnp.where(row < 3, 1.0, 0.0).astype(jnp.bfloat16)

    step = 16
    winds = wnd.reshape(levels * rows, lanes)

    def advance(top, bottom):
        above, _ = top
        below, last = bottom

        @pl.loop(0, levels // step)
        def _(i):
            here = pl.ds(pl.multiple_of(i * step, step), step)
            there = pl.ds(pl.multiple_of(levels + i * step, step), step)
            base = i * (step * rows)
            wide = lambda ref, index: ref[index, here, :].astype(jnp.float32)
            if edges:
                needed = (0, 1, 2, rows - 2, rows - 1)
                speeds = {r: row_of(winds, base + r, step, rows) for r in needed}
                speeds[rows] = wide(last, 2 * fields) + wide(last, 2 * fields + 1)
                groups = ((0, 2), (rows - 2, 2))
            else:
                speeds = {r: row_of(winds, base + r, step, rows) for r in range(2, rows - 1)}
                groups = ((2, 4),)
            for first, many in groups:
                faces = [face(speeds[first + j]) for j in range(many + 1)]
                for f in range(fields):
                    kept = lambda r: (mid[r - 2, f, here, :] if 2 <= r < rows - 2 else
                                      edg[r if r < 2 else r - rows + 4, f, here, :])
                    q = []
                    for r in range(first - 2, first + many + 2):
                        if r < 0:
                            q.append(wide(above, (r + 2) * fields + f))
                        elif r >= rows:
                            q.append(wide(below, (r - rows) * fields + f))
                        else:
                            q.append(kept(r))
                    for j, value in enumerate(rows_after(q, faces)):
                        if edges:
                            u, place = (0 if first == 0 else 1), j
                        else:
                            u, place = j // 2, j % 2
                        cols = pl.ds(place * lanes, lanes)
                        high = value.astype(jnp.bfloat16)
                        a[u, f, here, cols] = high
                        a[u, f, there, cols] = (value - high.astype(jnp.float32)).astype(jnp.bfloat16)

    if edges:
        by_parity(advance, (near2, near1), (far2, far1))
    else:
        advance((None, None), (None, None))

    starts = (0, rows - 2) if edges else (2, 4)
    flat = out.reshape(fields * levels * rows, lanes)

    def put(f, u, place, value):
        flat[pl.ds(f * levels * rows + starts[u] + place, levels, stride=rows), :] = value

    for u in range(2):
        for f in range(fields):
            both = jnp.dot(rcat[...], a[u, f], preferred_element_type=jnp.float32)
            value = both[:levels] + both[levels:]
            x[u, f * levels : (f + 1) * levels, :] = value.astype(jnp.bfloat16)
            if f == 0:
                rem[u] = value
            else:
                for place in range(2):
                    put(f, u, place, value[:, place * lanes : (place + 1) * lanes])
    lon = pl.ds(half * lanes, lanes)
    if last_half:
        store(out.at[most], out_hbm.at[most, :, :, lon])
    for u in range(2):
        net = network(x[u], w1, w2, g.at[u])
        for place in range(2):
            r = starts[u] + place
            lit = days[0, 0] == r * halves + half
            for i in range(1, days.shape[1]):
                lit = jnp.logical_or(lit, days[0, i] == r * halves + half)
            part = slice(place * lanes, (place + 1) * lanes)
            light = sun[r : r + 1, half * lanes : (half + 1) * lanes] * jnp.where(lit, 1.0, 0.0)
            put(0, u, place, rem[u, :, part] + net[:, part] * light)
    if last_half:
        store(out.at[0], out_hbm.at[0, :, :, lon])
    for made in stores:
        made.wait()


def finish(edges, half, halves, days, mid, edge_rows, wind, sun, rcat, w1, w2, *more):
    _, fields, levels, lanes = mid.shape
    rows = wind.shape[1]
    scratch = [
        pltpu.VMEM((2, fields, 2 * levels, 2 * lanes), jnp.bfloat16),
        pltpu.VMEM((2, w1.shape[1], 2 * lanes), jnp.bfloat16),
        pltpu.VMEM((2, levels, 2 * lanes), jnp.float32),
        pltpu.VMEM((2, w1.shape[0], 2 * lanes), jnp.bfloat16),
    ]
    operands = (days, mid, edge_rows, wind, sun, rcat, w1, w2) + more
    ins = [pl.BlockSpec(memory_space=pltpu.SMEM)] + [VMEM] * (len(operands) - 1)
    outs = [array((fields, levels, rows, lanes))]
    out_specs = [VMEM]
    alias = {12: 0} if edges else {}
    if edges and half == halves - 1:
        scratch.append(pltpu.SemaphoreType.DMA((halves + 1,)))
        outs = [array((fields, levels, rows, halves * lanes))] + outs
        out_specs = [HBM, VMEM]
        alias = {12: 1}
    return call(
        functools.partial(finish_kernel, edges, half, halves), f"finish_{'edges' if edges else 'inner'}{half}", outs,
        operands, ins=ins, out_specs=out_specs, scratch=scratch, alias=alias,
        limit=16, flops=2_000_000_000, moved=6_000_000)[0]


def shards(state, wind, sunlight, day_list, w_first, bias, w_second, remap):
    halves = state.shape[3] // LANES
    count = lax.axis_size("lat")
    near_route = [(i, i ^ 1) for i in range(count) if i ^ 1 < count]
    far_route = [(i, j) for i in range(count) for j in ((i - 1) if i % 2 == 0 else (i + 1),) if 0 <= j < count]
    every = range(halves)
    state = pltpu.with_memory_space_constraint(state, pltpu.HBM)
    wind = pltpu.with_memory_space_constraint(wind, pltpu.HBM)
    kept, winds, near, far, mid = [], [], [], [], []
    for h in every:
        k, w, near_sent, far_sent = pack(h, state, wind)
        kept.append(k)
        winds.append(w)
        far.append(lax.ppermute(far_sent, "lat", far_route))
        near.append(lax.ppermute(near_sent, "lat", near_route))
    for h in every:
        mid.append(inner(h, kept[h], winds[h]))
    w1, w2, rcat = weights(w_first, bias, w_second, remap)
    mid, w1, w2, rcat, near[0], far[0] = lax.optimization_barrier((mid, w1, w2, rcat, near[0], far[0]))
    edges, near2, far2, partial = [], [], [], []
    for h in every:
        rows, near_sent, far_sent = edge(h, kept[h], winds[h], near[h], far[h])
        edges.append(rows)
        far2.append(lax.ppermute(far_sent, "lat", far_route))
        near2.append(lax.ppermute(near_sent, "lat", near_route))
        partial.append(finish(False, h, halves, day_list, mid[h], rows, winds[h], sunlight, rcat, w1, w2))
        if h + 1 < halves:
            near[h + 1], far[h + 1], partial[h] = lax.optimization_barrier((near[h + 1], far[h + 1], partial[h]))
    near2[0], far2[0], partial = lax.optimization_barrier((near2[0], far2[0], partial))
    ready = ()
    for h in every:
        more = (near2[h], far2[h], near[h], far[h], partial[h])
        if h == halves - 1:
            more += ready
        done = finish(True, h, halves, day_list, mid[h], edges[h], winds[h], sunlight, rcat, w1, w2, *more)
        if h == halves - 1:
            return done
        ready += (done,)
        near2[h + 1], far2[h + 1], ready = lax.optimization_barrier((near2[h + 1], far2[h + 1], ready))


def solution(mesh):
    placed = (
        P("member", None, "lat", None),
        P("member", "lat", None),
        P(("member", "lat"), None),
        P(("member", "lat"), None),
        P(),
        P(),
        P(),
        P(),
    )
    return jax.shard_map(
        shards,
        mesh=mesh,
        in_specs=placed,
        out_specs=P("member", None, "lat", None),
        check_vma=False,
    )
```

```python
import functools
import jax
import jax.numpy as jnp
from jax import lax
from jax.experimental import pallas as pl
from jax.experimental.pallas import tpu as pltpu
from jax.sharding import PartitionSpec as P

LANES = 128
GELU_A = 0.7978845608028654
GELU_B = 0.7978845608028654 * 0.044715
HBM = pl.BlockSpec(memory_space=pltpu.HBM)
VMEM = pl.BlockSpec(memory_space=pltpu.VMEM)
MIB = 1024 * 1024


def call(kernel, name, outs, operands, ins=None, out_specs=None, scratch=(), limit=8, flops=0, moved=0, alias=None):
    return pl.pallas_call(
        kernel,
        in_specs=ins or [VMEM] * len(operands),
        out_specs=out_specs or [VMEM] * len(outs),
        out_shape=outs,
        scratch_shapes=scratch,
        input_output_aliases=alias or {},
        compiler_params=pltpu.CompilerParams(vmem_limit_bytes=limit * MIB),
        cost_estimate=pl.CostEstimate(flops=flops, bytes_accessed=moved, transcendentals=0),
        name=name,
    )(*operands)


def array(shape, dtype=jnp.float32):
    return jax.ShapeDtypeStruct(shape, dtype)


def limited(ahead, behind):
    return jnp.maximum(jnp.minimum(ahead, jnp.maximum(behind, 0.0)), jnp.minimum(behind, 0.0))


def face(speed):
    size = jnp.abs(speed)
    return speed > 0.0, speed, size * (0.5 - 0.5 * size)


def rows_after(q, faces):
    diffs = [b - a for a, b in zip(q[:-1], q[1:])]
    slopes = [None] + [limited(b, a) for a, b in zip(diffs[:-1], diffs[1:])]
    fluxes = []
    for j, (mask, speed, half) in enumerate(faces):
        edge = jnp.where(mask, q[j + 1], q[j + 2])
        slope = jnp.where(mask, slopes[j + 1], slopes[j + 2])
        fluxes.append(speed * edge + half * slope)
    return [q[j + 2] - (fluxes[j + 1] - fluxes[j]) for j in range(len(faces) - 1)]


def is_even():
    return lax.rem(lax.axis_index("lat"), 2) == 0


def by_parity(body, near, far):
    pl.when(is_even())(lambda: body(far, near))
    pl.when(jnp.logical_not(is_even()))(lambda: body(near, far))


def row_of(ref, start, count, rows):
    return ref[pl.ds(start, count, stride=rows), :]


def pack_kernel(half, parts, state_hbm, wind_hbm, kept_ref, winds_ref, near_ref, far_ref, sems):
    fields, levels, rows, lanes = kept_ref.shape
    size = levels // parts
    lon = pl.ds(half * lanes, lanes)
    copies = []
    for p in range(parts):
        some = pl.ds(p * size, size)
        made = pltpu.make_async_copy(state_hbm.at[:, some, :, lon], kept_ref.at[:, some], sems.at[p])
        made.start()
        copies.append(made)
    winds = pltpu.make_async_copy(wind_hbm.at[:, :, lon], winds_ref, sems.at[parts])
    winds.start()
    flat = kept_ref.reshape(fields * levels * rows, lanes)
    even = is_even()
    for p, made in enumerate(copies):
        made.wait()
        here = slice(p * size, (p + 1) * size)
        for f in range(fields):
            base = (f * levels + p * size) * rows
            for r in range(2):
                for ref, start in ((near_ref, jnp.where(even, rows - 2, 0)), (far_ref, jnp.where(even, 0, rows - 2))):
                    value = row_of(flat, base + start + r, size, rows)
                    ref[r * fields + f, here] = value.astype(jnp.bfloat16)
    winds.wait()
    speed = row_of(winds_ref.reshape(levels * rows, lanes), 0, levels, rows)
    high = speed.astype(jnp.bfloat16)
    low = (speed - high.astype(jnp.float32)).astype(jnp.bfloat16)
    for ref in (near_ref, far_ref):
        ref[2 * fields] = high
        ref[2 * fields + 1] = low


def pack(half, state, wind):
    fields, levels, rows, lons = state.shape
    parts = 4
    return call(
        functools.partial(pack_kernel, half, parts), f"pack{half}",
        [
            array((fields, levels, rows, LANES)),
            array((levels, rows, LANES)),
            array((2 * fields + 2, levels, LANES), jnp.bfloat16),
            array((2 * fields + 2, levels, LANES), jnp.bfloat16),
        ],
        (state, wind), ins=[HBM, HBM], scratch=[pltpu.SemaphoreType.DMA((parts + 1,))], moved=5_000_000)


def inner_kernel(kept_ref, winds_ref, out_ref):
    fields, levels, rows, lanes = kept_ref.shape
    step = 8
    flat = kept_ref.reshape(fields * levels * rows, lanes)
    winds = winds_ref.reshape(levels * rows, lanes)

    @pl.loop(0, levels // step)
    def _(i):
        base = i * (step * rows)
        faces = [face(row_of(winds, base + r, step, rows)) for r in range(2, rows - 1)]
        level = pl.multiple_of(i * step, step)
        for f in range(fields):
            q = [row_of(flat, f * levels * rows + base + r, step, rows) for r in range(rows)]
            for r, value in enumerate(rows_after(q, faces)):
                out_ref[r, f, pl.ds(level, step), :] = value


def inner(half, kept, winds):
    fields, levels, rows, lanes = kept.shape
    return call(
        inner_kernel, f"inner{half}", [array((rows - 4, fields, levels, lanes))], (kept, winds),
        flops=50_000_000, moved=4_000_000)[0]


def edge_kernel(kept_ref, winds_ref, near_in, far_in, out_ref, near_out, far_out):
    fields, levels, rows, lanes = kept_ref.shape
    step = 16
    flat = kept_ref.reshape(fields * levels * rows, lanes)
    winds = winds_ref.reshape(levels * rows, lanes)

    def body(top, bottom):
        above_ref, down_ref = top
        below_ref, up_ref = bottom

        @pl.loop(0, levels // step)
        def _(i):
            base = i * (step * rows)
            here = pl.ds(pl.multiple_of(i * step, step), step)
            wide = lambda ref, index: ref[index, here, :].astype(jnp.float32)
            speeds = {r: row_of(winds, base + r, step, rows) for r in (0, 1, 2, rows - 2, rows - 1)}
            speeds[rows] = wide(below_ref, 2 * fields) + wide(below_ref, 2 * fields + 1)
            for side, first in enumerate((0, rows - 2)):
                faces = [face(speeds[first + j]) for j in range(3)]
                for f in range(fields):
                    own = lambda r: row_of(flat, f * levels * rows + base + r, step, rows)
                    if side == 0:
                        q = [wide(above_ref, f), wide(above_ref, fields + f)] + [own(r) for r in range(4)]
                    else:
                        q = [own(r) for r in range(rows - 4, rows)] + [wide(below_ref, f), wide(below_ref, fields + f)]
                    sent = (down_ref, up_ref)[side]
                    for r, value in enumerate(rows_after(q, faces)):
                        out_ref[2 * side + r, f, here, :] = value
                        sent[r * fields + f, here, :] = value.astype(jnp.bfloat16)

    by_parity(body, (near_in, near_out), (far_in, far_out))


def edge(half, kept, winds, near, far):
    fields, levels, rows, lanes = kept.shape
    sent = array((2 * fields, levels, lanes), jnp.bfloat16)
    return call(
        edge_kernel, f"edge{half}", [array((4, fields, levels, lanes)), sent, sent],
        (kept, winds, near, far), flops=50_000_000, moved=5_000_000)


def weights_kernel(first_ref, bias_ref, second_ref, remap_ref, first_out, second_out, split_out):
    inputs, hidden = first_ref.shape
    levels = remap_ref.shape[0]
    whole = remap_ref[...]
    r_high = whole.astype(jnp.bfloat16)
    r_low = (whole - r_high.astype(jnp.float32)).astype(jnp.bfloat16)
    for j in range(2):
        split_out[:levels, j * levels : (j + 1) * levels] = r_high
        split_out[levels:, j * levels : (j + 1) * levels] = r_low
    chunk = 256
    same = lambda d: lax.broadcasted_iota(jnp.int32, (chunk, chunk), d)
    unit = jnp.where(same(0) == same(1), 1.0, 0.0).astype(jnp.bfloat16)
    flip = lambda part: lax.dot_general(
        unit, part, (((1,), (1,)), ((), ())), preferred_element_type=jnp.float32).astype(jnp.bfloat16)
    small = unit[:LANES, :LANES]
    row = lax.broadcasted_iota(jnp.int32, (LANES, chunk), 0)
    for j in range(hidden // chunk):
        here = slice(j * chunk, (j + 1) * chunk)
        first_out[here, :inputs] = flip(first_ref[:, here])
        bias = bias_ref[:, here]
        high = bias.astype(jnp.bfloat16).astype(jnp.float32)
        middle = (bias - high).astype(jnp.bfloat16).astype(jnp.float32)
        low = bias - high - middle
        stacked = jnp.where(row == 0, high, jnp.where(row == 1, middle, jnp.where(row == 2, low, 0.0)))
        first_out[here, inputs:] = flip(stacked.astype(jnp.bfloat16))
        second_out[:, here] = lax.dot_general(
            small, second_ref[here, :], (((1,), (1,)), ((), ())),
            preferred_element_type=jnp.float32).astype(jnp.bfloat16)


def weights(w_first, bias, w_second, remap):
    inputs, hidden = w_first.shape
    levels = remap.shape[0]
    outputs = w_second.shape[1]
    return call(
        weights_kernel, "weights",
        [
            array((hidden, inputs + LANES), jnp.bfloat16),
            array((outputs, hidden), jnp.bfloat16),
            array((2 * levels, 2 * levels), jnp.bfloat16),
        ],
        (w_first, bias.reshape(1, hidden), w_second, remap), flops=50_000_000, moved=7_000_000)


def network(x, w1_ref, w2_ref, g_ref):
    hidden = w1_ref.shape[0]
    chunk = 512
    for c in range(hidden // chunk):
        here = slice(c * chunk, (c + 1) * chunk)
        v = jnp.dot(w1_ref[here, :], x, preferred_element_type=jnp.float32)
        h = 0.5 * v
        t = jnp.tanh(v * (GELU_A + GELU_B * (v * v)))
        g_ref[here, :] = (h + h * t).astype(jnp.bfloat16)
    return jnp.dot(w2_ref[...], g_ref[...], preferred_element_type=jnp.float32)


def finish_kernel(edges, half, halves, *refs):
    last_half = edges and half == halves - 1
    if last_half:
        (days, mid, edg, wnd, sun, rcat, w1, w2, near2, far2, near1, far1, _, *refs) = refs
        *ready, out_hbm, out, a, x, rem, g, sems = refs
    elif edges:
        (days, mid, edg, wnd, sun, rcat, w1, w2, near2, far2, near1, far1, _, out, a, x, rem, g) = refs
    else:
        (days, mid, edg, wnd, sun, rcat, w1, w2, out, a, x, rem, g) = refs
    _, fields, levels, lanes = mid.shape
    rows = wnd.shape[1]
    inputs = fields * levels
    most = pl.ds(1, fields - 1)
    stores = []

    def store(source, target):
        made = pltpu.make_async_copy(source, target, sems.at[len(stores)])
        made.start()
        stores.append(made)

    if last_half:
        for h, source in enumerate(ready):
            store(source, out_hbm.at[:, :, :, pl.ds(h * lanes, lanes)])
    row = lax.broadcasted_iota(jnp.int32, (x.shape[1] - inputs, x.shape[2]), 0)
    for u in range(2):
        x[u, inputs:, :] = jnp.where(row < 3, 1.0, 0.0).astype(jnp.bfloat16)

    step = 16
    winds = wnd.reshape(levels * rows, lanes)

    def advance(top, bottom):
        above, _ = top
        below, last = bottom

        @pl.loop(0, levels // step)
        def _(i):
            here = pl.ds(pl.multiple_of(i * step, step), step)
            there = pl.ds(pl.multiple_of(levels + i * step, step), step)
            base = i * (step * rows)
            wide = lambda ref, index: ref[index, here, :].astype(jnp.float32)
            if edges:
                needed = (0, 1, 2, rows - 2, rows - 1)
                speeds = {r: row_of(winds, base + r, step, rows) for r in needed}
                speeds[rows] = wide(last, 2 * fields) + wide(last, 2 * fields + 1)
                groups = ((0, 2), (rows - 2, 2))
            else:
                speeds = {r: row_of(winds, base + r, step, rows) for r in range(2, rows - 1)}
                groups = ((2, 4),)
            for first, many in groups:
                faces = [face(speeds[first + j]) for j in range(many + 1)]
                for f in range(fields):
                    kept = lambda r: (mid[r - 2, f, here, :] if 2 <= r < rows - 2 else
                                      edg[r if r < 2 else r - rows + 4, f, here, :])
                    q = []
                    for r in range(first - 2, first + many + 2):
                        if r < 0:
                            q.append(wide(above, (r + 2) * fields + f))
                        elif r >= rows:
                            q.append(wide(below, (r - rows) * fields + f))
                        else:
                            q.append(kept(r))
                    for j, value in enumerate(rows_after(q, faces)):
                        if edges:
                            u, place = (0 if first == 0 else 1), j
                        else:
                            u, place = j // 2, j % 2
                        cols = pl.ds(place * lanes, lanes)
                        high = value.astype(jnp.bfloat16)
                        a[u, f, here, cols] = high
                        a[u, f, there, cols] = (value - high.astype(jnp.float32)).astype(jnp.bfloat16)

    if edges:
        by_parity(advance, (near2, near1), (far2, far1))
    else:
        advance((None, None), (None, None))

    starts = (0, rows - 2) if edges else (2, 4)
    flat = out.reshape(fields * levels * rows, lanes)

    def put(f, u, place, value):
        flat[pl.ds(f * levels * rows + starts[u] + place, levels, stride=rows), :] = value

    for u in range(2):
        for f in range(fields):
            both = jnp.dot(rcat[...], a[u, f], preferred_element_type=jnp.float32)
            value = both[:levels] + both[levels:]
            x[u, f * levels : (f + 1) * levels, :] = value.astype(jnp.bfloat16)
            if f == 0:
                rem[u] = value
            else:
                for place in range(2):
                    put(f, u, place, value[:, place * lanes : (place + 1) * lanes])
    lon = pl.ds(half * lanes, lanes)
    if last_half:
        store(out.at[most], out_hbm.at[most, :, :, lon])
    for u in range(2):
        net = network(x[u], w1, w2, g.at[u])
        for place in range(2):
            r = starts[u] + place
            lit = days[0, 0] == r * halves + half
            for i in range(1, days.shape[1]):
                lit = jnp.logical_or(lit, days[0, i] == r * halves + half)
            part = slice(place * lanes, (place + 1) * lanes)
            light = sun[r : r + 1, half * lanes : (half + 1) * lanes] * jnp.where(lit, 1.0, 0.0)
            put(0, u, place, rem[u, :, part] + net[:, part] * light)
    if last_half:
        store(out.at[0], out_hbm.at[0, :, :, lon])
    for made in stores:
        made.wait()


def finish(edges, half, halves, days, mid, edge_rows, wind, sun, rcat, w1, w2, *more):
    _, fields, levels, lanes = mid.shape
    rows = wind.shape[1]
    scratch = [
        pltpu.VMEM((2, fields, 2 * levels, 2 * lanes), jnp.bfloat16),
        pltpu.VMEM((2, w1.shape[1], 2 * lanes), jnp.bfloat16),
        pltpu.VMEM((2, levels, 2 * lanes), jnp.float32),
        pltpu.VMEM((2, w1.shape[0], 2 * lanes), jnp.bfloat16),
    ]
    operands = (days, mid, edge_rows, wind, sun, rcat, w1, w2) + more
    ins = [pl.BlockSpec(memory_space=pltpu.SMEM)] + [VMEM] * (len(operands) - 1)
    outs = [array((fields, levels, rows, lanes))]
    out_specs = [VMEM]
    alias = {12: 0} if edges else {}
    if edges and half == halves - 1:
        scratch.append(pltpu.SemaphoreType.DMA((halves + 1,)))
        outs = [array((fields, levels, rows, halves * lanes))] + outs
        out_specs = [HBM, VMEM]
        alias = {12: 1}
    return call(
        functools.partial(finish_kernel, edges, half, halves), f"finish_{'edges' if edges else 'inner'}{half}", outs,
        operands, ins=ins, out_specs=out_specs, scratch=scratch, alias=alias,
        limit=16, flops=2_000_000_000, moved=6_000_000)[0]


def shards(state, wind, sunlight, day_list, w_first, bias, w_second, remap):
    halves = state.shape[3] // LANES
    count = lax.axis_size("lat")
    near_route = [(i, i ^ 1) for i in range(count) if i ^ 1 < count]
    far_route = [(i, j) for i in range(count) for j in ((i - 1) if i % 2 == 0 else (i + 1),) if 0 <= j < count]
    every = range(halves)
    kept, winds, near, far, mid = [], [], [], [], []
    for h in every:
        k, w, near_sent, far_sent = pack(
            h, pltpu.with_memory_space_constraint(state, pltpu.HBM), pltpu.with_memory_space_constraint(wind, pltpu.HBM))
        kept.append(k)
        winds.append(w)
        far.append(lax.ppermute(far_sent, "lat", far_route))
        near.append(lax.ppermute(near_sent, "lat", near_route))
        mid.append(inner(h, k, w))
        if h == 0:
            w1, w2, rcat = weights(w_first, bias, w_second, remap)
            wind, w1, w2, rcat, mid[0] = lax.optimization_barrier((wind, w1, w2, rcat, mid[0]))
        else:
            near[0], far[0], near_sent, far_sent = lax.optimization_barrier((near[0], far[0], near_sent, far_sent))
    edges, near2, far2, partial = [], [], [], []
    for h in every:
        rows, near_sent, far_sent = edge(h, kept[h], winds[h], near[h], far[h])
        edges.append(rows)
        far2.append(lax.ppermute(far_sent, "lat", far_route))
        near2.append(lax.ppermute(near_sent, "lat", near_route))
        partial.append(finish(False, h, halves, day_list, mid[h], rows, winds[h], sunlight, rcat, w1, w2))
        if h + 1 < halves:
            near[h + 1], far[h + 1], partial[h] = lax.optimization_barrier((near[h + 1], far[h + 1], partial[h]))
    near2[0], far2[0], partial = lax.optimization_barrier((near2[0], far2[0], partial))
    ready = ()
    for h in every:
        more = (near2[h], far2[h], near[h], far[h], partial[h])
        if h == halves - 1:
            more += ready
        done = finish(True, h, halves, day_list, mid[h], edges[h], winds[h], sunlight, rcat, w1, w2, *more)
        if h == halves - 1:
            return done
        ready += (done,)
        near2[h + 1], far2[h + 1], ready = lax.optimization_barrier((near2[h + 1], far2[h + 1], ready))


def solution(mesh):
    placed = (
        P("member", None, "lat", None),
        P("member", "lat", None),
        P(("member", "lat"), None),
        P(("member", "lat"), None),
        P(),
        P(),
        P(),
        P(),
    )
    return jax.shard_map(
        shards,
        mesh=mesh,
        in_specs=placed,
        out_specs=P("member", None, "lat", None),
        check_vma=False,
    )
```

```python
import functools
import jax
import jax.numpy as jnp
from jax import lax
from jax.experimental import pallas as pl
from jax.experimental.pallas import tpu as pltpu
from jax.sharding import PartitionSpec as P

LANES = 128
CODE = 80.0
GELU_A = 0.7978845608028654
GELU_B = 0.7978845608028654 * 0.044715
HBM = pl.BlockSpec(memory_space=pltpu.HBM)
VMEM = pl.BlockSpec(memory_space=pltpu.VMEM)
MIB = 1024 * 1024


def call(kernel, name, outs, operands, ins=None, out_specs=None, scratch=(), limit=8, flops=0, moved=0, alias=None):
    return pl.pallas_call(
        kernel,
        in_specs=ins or [VMEM] * len(operands),
        out_specs=out_specs or [VMEM] * len(outs),
        out_shape=outs,
        scratch_shapes=scratch,
        input_output_aliases=alias or {},
        compiler_params=pltpu.CompilerParams(vmem_limit_bytes=limit * MIB),
        cost_estimate=pl.CostEstimate(flops=flops, bytes_accessed=moved, transcendentals=0),
        name=name,
    )(*operands)


def array(shape, dtype=jnp.float32):
    return jax.ShapeDtypeStruct(shape, dtype)


def limited(ahead, behind):
    return jnp.maximum(jnp.minimum(ahead, jnp.maximum(behind, 0.0)), jnp.minimum(behind, 0.0))


def face(speed):
    size = jnp.abs(speed)
    return speed > 0.0, speed, size * (0.5 - 0.5 * size)


def rows_after(q, faces):
    diffs = [b - a for a, b in zip(q[:-1], q[1:])]
    slopes = [None] + [limited(b, a) for a, b in zip(diffs[:-1], diffs[1:])]
    fluxes = []
    for j, (mask, speed, half) in enumerate(faces):
        edge = jnp.where(mask, q[j + 1], q[j + 2])
        slope = jnp.where(mask, slopes[j + 1], slopes[j + 2])
        fluxes.append(speed * edge + half * slope)
    return [q[j + 2] - (fluxes[j + 1] - fluxes[j]) for j in range(len(faces) - 1)]


def encode(speed):
    size = jnp.exp(CODE * jnp.abs(speed))
    return jnp.where(speed < 0.0, -size, size).astype(jnp.bfloat16)


def decode(code):
    size = jnp.log(jnp.maximum(jnp.abs(code), 1.0)) * (1.0 / CODE)
    return jnp.where(code < 0.0, -size, size)


def is_even():
    return lax.rem(lax.axis_index("lat"), 2) == 0


def by_parity(body, near, far):
    pl.when(is_even())(lambda: body(far, near))
    pl.when(jnp.logical_not(is_even()))(lambda: body(near, far))


def row_of(ref, start, count, rows):
    return ref[pl.ds(start, count, stride=rows), :]


def pack_kernel(half, parts, state_hbm, wind_hbm, kept_ref, winds_ref, near_ref, far_ref, sems):
    fields, levels, rows, lanes = kept_ref.shape
    size = levels // parts
    lon = pl.ds(half * lanes, lanes)
    copies = []
    for p in range(parts):
        some = pl.ds(p * size, size)
        made = pltpu.make_async_copy(state_hbm.at[:, some, :, lon], kept_ref.at[:, some], sems.at[p])
        made.start()
        copies.append(made)
    winds = pltpu.make_async_copy(wind_hbm.at[:, :, lon], winds_ref, sems.at[parts])
    winds.start()
    flat = kept_ref.reshape(fields * levels * rows, lanes)
    even = is_even()
    for p, made in enumerate(copies):
        made.wait()
        here = slice(p * size, (p + 1) * size)
        for f in range(fields):
            base = (f * levels + p * size) * rows
            for r in range(2):
                for ref, start in ((near_ref, jnp.where(even, rows - 2, 0)), (far_ref, jnp.where(even, 0, rows - 2))):
                    value = row_of(flat, base + start + r, size, rows)
                    ref[r * fields + f, here] = value.astype(jnp.bfloat16)
    winds.wait()
    speed = row_of(winds_ref.reshape(levels * rows, lanes), 0, levels, rows)
    code = encode(speed)
    for ref in (near_ref, far_ref):
        ref[2 * fields] = code


def pack(half, state, wind):
    fields, levels, rows, lons = state.shape
    parts = 4
    return call(
        functools.partial(pack_kernel, half, parts), f"pack{half}",
        [
            array((fields, levels, rows, LANES)),
            array((levels, rows, LANES)),
            array((2 * fields + 1, levels, LANES), jnp.bfloat16),
            array((2 * fields + 1, levels, LANES), jnp.bfloat16),
        ],
        (state, wind), ins=[HBM, HBM], scratch=[pltpu.SemaphoreType.DMA((parts + 1,))], moved=5_000_000)


def inner_kernel(kept_ref, winds_ref, out_ref):
    fields, levels, rows, lanes = kept_ref.shape
    step = 8
    flat = kept_ref.reshape(fields * levels * rows, lanes)
    winds = winds_ref.reshape(levels * rows, lanes)

    @pl.loop(0, levels // step)
    def _(i):
        base = i * (step * rows)
        faces = [face(row_of(winds, base + r, step, rows)) for r in range(2, rows - 1)]
        level = pl.multiple_of(i * step, step)
        for f in range(fields):
            q = [row_of(flat, f * levels * rows + base + r, step, rows) for r in range(rows)]
            for r, value in enumerate(rows_after(q, faces)):
                out_ref[r, f, pl.ds(level, step), :] = value


def inner(half, kept, winds):
    fields, levels, rows, lanes = kept.shape
    return call(
        inner_kernel, f"inner{half}", [array((rows - 4, fields, levels, lanes))], (kept, winds),
        flops=50_000_000, moved=4_000_000)[0]


def edge_kernel(kept_ref, winds_ref, near_in, far_in, out_ref, near_out, far_out):
    fields, levels, rows, lanes = kept_ref.shape
    step = 16
    flat = kept_ref.reshape(fields * levels * rows, lanes)
    winds = winds_ref.reshape(levels * rows, lanes)

    def body(top, bottom):
        above_ref, down_ref = top
        below_ref, up_ref = bottom

        @pl.loop(0, levels // step)
        def _(i):
            base = i * (step * rows)
            here = pl.ds(pl.multiple_of(i * step, step), step)
            wide = lambda ref, index: ref[index, here, :].astype(jnp.float32)
            speeds = {r: row_of(winds, base + r, step, rows) for r in (0, 1, 2, rows - 2, rows - 1)}
            speeds[rows] = decode(wide(below_ref, 2 * fields))
            for side, first in enumerate((0, rows - 2)):
                faces = [face(speeds[first + j]) for j in range(3)]
                for f in range(fields):
                    own = lambda r: row_of(flat, f * levels * rows + base + r, step, rows)
                    if side == 0:
                        q = [wide(above_ref, f), wide(above_ref, fields + f)] + [own(r) for r in range(4)]
                    else:
                        q = [own(r) for r in range(rows - 4, rows)] + [wide(below_ref, f), wide(below_ref, fields + f)]
                    sent = (down_ref, up_ref)[side]
                    for r, value in enumerate(rows_after(q, faces)):
                        out_ref[2 * side + r, f, here, :] = value
                        sent[r * fields + f, here, :] = value.astype(jnp.bfloat16)

    by_parity(body, (near_in, near_out), (far_in, far_out))


def edge(half, kept, winds, near, far):
    fields, levels, rows, lanes = kept.shape
    sent = array((2 * fields, levels, lanes), jnp.bfloat16)
    return call(
        edge_kernel, f"edge{half}", [array((4, fields, levels, lanes)), sent, sent],
        (kept, winds, near, far), flops=50_000_000, moved=5_000_000)


def weights_kernel(first_ref, bias_ref, second_ref, remap_ref, first_out, second_out, split_out):
    inputs, hidden = first_ref.shape
    levels = remap_ref.shape[0]
    whole = remap_ref[...]
    r_high = whole.astype(jnp.bfloat16)
    r_low = (whole - r_high.astype(jnp.float32)).astype(jnp.bfloat16)
    for j in range(2):
        split_out[:levels, j * levels : (j + 1) * levels] = r_high
        split_out[levels:, j * levels : (j + 1) * levels] = r_low
    chunk = 256
    same = lambda d: lax.broadcasted_iota(jnp.int32, (chunk, chunk), d)
    unit = jnp.where(same(0) == same(1), 1.0, 0.0).astype(jnp.bfloat16)
    flip = lambda part: lax.dot_general(
        unit, part, (((1,), (1,)), ((), ())), preferred_element_type=jnp.float32).astype(jnp.bfloat16)
    small = unit[:LANES, :LANES]
    row = lax.broadcasted_iota(jnp.int32, (LANES, chunk), 0)
    for j in range(hidden // chunk):
        here = slice(j * chunk, (j + 1) * chunk)
        first_out[here, :inputs] = flip(first_ref[:, here])
        bias = bias_ref[:, here]
        high = bias.astype(jnp.bfloat16).astype(jnp.float32)
        middle = (bias - high).astype(jnp.bfloat16).astype(jnp.float32)
        low = bias - high - middle
        stacked = jnp.where(row == 0, high, jnp.where(row == 1, middle, jnp.where(row == 2, low, 0.0)))
        first_out[here, inputs:] = flip(stacked.astype(jnp.bfloat16))
        second_out[:, here] = lax.dot_general(
            small, second_ref[here, :], (((1,), (1,)), ((), ())),
            preferred_element_type=jnp.float32).astype(jnp.bfloat16)


def weights(w_first, bias, w_second, remap):
    inputs, hidden = w_first.shape
    levels = remap.shape[0]
    outputs = w_second.shape[1]
    return call(
        weights_kernel, "weights",
        [
            array((hidden, inputs + LANES), jnp.bfloat16),
            array((outputs, hidden), jnp.bfloat16),
            array((2 * levels, 2 * levels), jnp.bfloat16),
        ],
        (w_first, bias.reshape(1, hidden), w_second, remap), flops=50_000_000, moved=7_000_000)


def network(x, w1_ref, w2_ref, g_ref):
    hidden = w1_ref.shape[0]
    chunk = 512
    for c in range(hidden // chunk):
        here = slice(c * chunk, (c + 1) * chunk)
        v = jnp.dot(w1_ref[here, :], x, preferred_element_type=jnp.float32)
        h = 0.5 * v
        t = jnp.tanh(v * (GELU_A + GELU_B * (v * v)))
        g_ref[here, :] = (h + h * t).astype(jnp.bfloat16)
    return jnp.dot(w2_ref[...], g_ref[...], preferred_element_type=jnp.float32)


def finish_kernel(edges, half, halves, *refs):
    last_half = edges and half == halves - 1
    if last_half:
        (days, mid, edg, wnd, sun, rcat, w1, w2, near2, far2, near1, far1, _, *refs) = refs
        *ready, out_hbm, out, a, x, rem, g, sems = refs
    elif edges:
        (days, mid, edg, wnd, sun, rcat, w1, w2, near2, far2, near1, far1, _, out, a, x, rem, g) = refs
    else:
        (days, mid, edg, wnd, sun, rcat, w1, w2, out, a, x, rem, g) = refs
    _, fields, levels, lanes = mid.shape
    rows = wnd.shape[1]
    inputs = fields * levels
    most = pl.ds(1, fields - 1)
    stores = []

    def store(source, target):
        made = pltpu.make_async_copy(source, target, sems.at[len(stores)])
        made.start()
        stores.append(made)

    if last_half:
        for h, source in enumerate(ready):
            store(source, out_hbm.at[:, :, :, pl.ds(h * lanes, lanes)])
    row = lax.broadcasted_iota(jnp.int32, (x.shape[1] - inputs, x.shape[2]), 0)
    for u in range(2):
        x[u, inputs:, :] = jnp.where(row < 3, 1.0, 0.0).astype(jnp.bfloat16)

    step = 16
    winds = wnd.reshape(levels * rows, lanes)

    def advance(top, bottom):
        above, _ = top
        below, last = bottom

        @pl.loop(0, levels // step)
        def _(i):
            here = pl.ds(pl.multiple_of(i * step, step), step)
            there = pl.ds(pl.multiple_of(levels + i * step, step), step)
            base = i * (step * rows)
            wide = lambda ref, index: ref[index, here, :].astype(jnp.float32)
            if edges:
                needed = (0, 1, 2, rows - 2, rows - 1)
                speeds = {r: row_of(winds, base + r, step, rows) for r in needed}
                speeds[rows] = decode(wide(last, 2 * fields))
                groups = ((0, 2), (rows - 2, 2))
            else:
                speeds = {r: row_of(winds, base + r, step, rows) for r in range(2, rows - 1)}
                groups = ((2, 4),)
            for first, many in groups:
                faces = [face(speeds[first + j]) for j in range(many + 1)]
                for f in range(fields):
                    kept = lambda r: (mid[r - 2, f, here, :] if 2 <= r < rows - 2 else
                                      edg[r if r < 2 else r - rows + 4, f, here, :])
                    q = []
                    for r in range(first - 2, first + many + 2):
                        if r < 0:
                            q.append(wide(above, (r + 2) * fields + f))
                        elif r >= rows:
                            q.append(wide(below, (r - rows) * fields + f))
                        else:
                            q.append(kept(r))
                    for j, value in enumerate(rows_after(q, faces)):
                        if edges:
                            u, place = (0 if first == 0 else 1), j
                        else:
                            u, place = j // 2, j % 2
                        cols = pl.ds(place * lanes, lanes)
                        high = value.astype(jnp.bfloat16)
                        a[u, f, here, cols] = high
                        a[u, f, there, cols] = (value - high.astype(jnp.float32)).astype(jnp.bfloat16)

    if edges:
        by_parity(advance, (near2, near1), (far2, far1))
    else:
        advance((None, None), (None, None))

    starts = (0, rows - 2) if edges else (2, 4)
    flat = out.reshape(fields * levels * rows, lanes)

    def put(f, u, place, value):
        flat[pl.ds(f * levels * rows + starts[u] + place, levels, stride=rows), :] = value

    for u in range(2):
        for f in range(fields):
            both = jnp.dot(rcat[...], a[u, f], preferred_element_type=jnp.float32)
            value = both[:levels] + both[levels:]
            x[u, f * levels : (f + 1) * levels, :] = value.astype(jnp.bfloat16)
            if f == 0:
                rem[u] = value
            else:
                for place in range(2):
                    put(f, u, place, value[:, place * lanes : (place + 1) * lanes])
    lon = pl.ds(half * lanes, lanes)
    if last_half:
        store(out.at[most], out_hbm.at[most, :, :, lon])
    for u in range(2):
        net = network(x[u], w1, w2, g.at[u])
        for place in range(2):
            r = starts[u] + place
            lit = days[0, 0] == r * halves + half
            for i in range(1, days.shape[1]):
                lit = jnp.logical_or(lit, days[0, i] == r * halves + half)
            part = slice(place * lanes, (place + 1) * lanes)
            light = sun[r : r + 1, half * lanes : (half + 1) * lanes] * jnp.where(lit, 1.0, 0.0)
            put(0, u, place, rem[u, :, part] + net[:, part] * light)
    if last_half:
        store(out.at[0], out_hbm.at[0, :, :, lon])
    for made in stores:
        made.wait()


def finish(edges, half, halves, days, mid, edge_rows, wind, sun, rcat, w1, w2, *more):
    _, fields, levels, lanes = mid.shape
    rows = wind.shape[1]
    scratch = [
        pltpu.VMEM((2, fields, 2 * levels, 2 * lanes), jnp.bfloat16),
        pltpu.VMEM((2, w1.shape[1], 2 * lanes), jnp.bfloat16),
        pltpu.VMEM((2, levels, 2 * lanes), jnp.float32),
        pltpu.VMEM((2, w1.shape[0], 2 * lanes), jnp.bfloat16),
    ]
    operands = (days, mid, edge_rows, wind, sun, rcat, w1, w2) + more
    ins = [pl.BlockSpec(memory_space=pltpu.SMEM)] + [VMEM] * (len(operands) - 1)
    outs = [array((fields, levels, rows, lanes))]
    out_specs = [VMEM]
    alias = {12: 0} if edges else {}
    if edges and half == halves - 1:
        scratch.append(pltpu.SemaphoreType.DMA((halves + 1,)))
        outs = [array((fields, levels, rows, halves * lanes))] + outs
        out_specs = [HBM, VMEM]
        alias = {12: 1}
    return call(
        functools.partial(finish_kernel, edges, half, halves), f"finish_{'edges' if edges else 'inner'}{half}", outs,
        operands, ins=ins, out_specs=out_specs, scratch=scratch, alias=alias,
        limit=16, flops=2_000_000_000, moved=6_000_000)[0]


def shards(state, wind, sunlight, day_list, w_first, bias, w_second, remap):
    halves = state.shape[3] // LANES
    count = lax.axis_size("lat")
    near_route = [(i, i ^ 1) for i in range(count) if i ^ 1 < count]
    far_route = [(i, j) for i in range(count) for j in ((i - 1) if i % 2 == 0 else (i + 1),) if 0 <= j < count]
    every = range(halves)
    kept, winds, near, far, mid = [], [], [], [], []
    for h in every:
        k, w, near_sent, far_sent = pack(
            h, pltpu.with_memory_space_constraint(state, pltpu.HBM), pltpu.with_memory_space_constraint(wind, pltpu.HBM))
        kept.append(k)
        winds.append(w)
        far.append(lax.ppermute(far_sent, "lat", far_route))
        near.append(lax.ppermute(near_sent, "lat", near_route))
        mid.append(inner(h, k, w))
        if h == 0:
            wind, mid[0] = lax.optimization_barrier((wind, mid[0]))
        elif h == 1:
            w_first, near_sent = lax.optimization_barrier((w_first, near_sent))
    w1, w2, rcat = weights(w_first, bias, w_second, remap)
    near[0], far[0], mid, w1, w2, rcat = lax.optimization_barrier((near[0], far[0], mid, w1, w2, rcat))
    edges, near2, far2, partial = [], [], [], []
    for h in every:
        rows, near_sent, far_sent = edge(h, kept[h], winds[h], near[h], far[h])
        edges.append(rows)
        far2.append(lax.ppermute(far_sent, "lat", far_route))
        near2.append(lax.ppermute(near_sent, "lat", near_route))
        partial.append(finish(False, h, halves, day_list, mid[h], rows, winds[h], sunlight, rcat, w1, w2))
        if h + 1 < halves:
            near[h + 1], far[h + 1], partial[h] = lax.optimization_barrier((near[h + 1], far[h + 1], partial[h]))
    near2[0], far2[0], partial = lax.optimization_barrier((near2[0], far2[0], partial))
    ready = ()
    for h in every:
        more = (near2[h], far2[h], near[h], far[h], partial[h])
        if h == halves - 1:
            more += ready
        done = finish(True, h, halves, day_list, mid[h], edges[h], winds[h], sunlight, rcat, w1, w2, *more)
        if h == halves - 1:
            return done
        ready += (done,)
        near2[h + 1], far2[h + 1], ready = lax.optimization_barrier((near2[h + 1], far2[h + 1], ready))


def solution(mesh):
    placed = (
        P("member", None, "lat", None),
        P("member", "lat", None),
        P(("member", "lat"), None),
        P(("member", "lat"), None),
        P(),
        P(),
        P(),
        P(),
    )
    return jax.shard_map(
        shards,
        mesh=mesh,
        in_specs=placed,
        out_specs=P("member", None, "lat", None),
        check_vma=False,
    )
```

```python
import functools
import jax
import jax.numpy as jnp
from jax import lax
from jax.experimental import pallas as pl
from jax.experimental.pallas import tpu as pltpu
from jax.sharding import PartitionSpec as P

LANES = 128
CODE = 80.0
GELU_A = 0.7978845608028654
GELU_B = 0.7978845608028654 * 0.044715
HBM = pl.BlockSpec(memory_space=pltpu.HBM)
VMEM = pl.BlockSpec(memory_space=pltpu.VMEM)
MIB = 1024 * 1024


def call(kernel, outs, operands, ins=None, out_specs=None, scratch=(), limit=8, flops=0, moved=0, alias=None):
    return pl.pallas_call(
        kernel,
        in_specs=ins or [VMEM] * len(operands),
        out_specs=out_specs or [VMEM] * len(outs),
        out_shape=outs,
        scratch_shapes=scratch,
        input_output_aliases=alias or {},
        compiler_params=pltpu.CompilerParams(vmem_limit_bytes=limit * MIB),
        cost_estimate=pl.CostEstimate(flops=flops, bytes_accessed=moved, transcendentals=0),
    )(*operands)


def array(shape, dtype=jnp.float32):
    return jax.ShapeDtypeStruct(shape, dtype)


def limited(ahead, behind):
    return jnp.maximum(jnp.minimum(ahead, jnp.maximum(behind, 0.0)), jnp.minimum(behind, 0.0))


def face(speed):
    size = jnp.abs(speed)
    return speed > 0.0, speed, size * (0.5 - 0.5 * size)


def rows_after(q, faces):
    diffs = [b - a for a, b in zip(q[:-1], q[1:])]
    slopes = [None] + [limited(b, a) for a, b in zip(diffs[:-1], diffs[1:])]
    fluxes = []
    for j, (mask, speed, half) in enumerate(faces):
        edge = jnp.where(mask, q[j + 1], q[j + 2])
        slope = jnp.where(mask, slopes[j + 1], slopes[j + 2])
        fluxes.append(speed * edge + half * slope)
    return [q[j + 2] - (fluxes[j + 1] - fluxes[j]) for j in range(len(faces) - 1)]


def encode(speed):
    size = jnp.exp(CODE * jnp.abs(speed))
    return jnp.where(speed < 0.0, -size, size).astype(jnp.bfloat16)


def decode(code):
    size = jnp.log(jnp.maximum(jnp.abs(code), 1.0)) * (1.0 / CODE)
    return jnp.where(code < 0.0, -size, size)


def is_even():
    return lax.rem(lax.axis_index("lat"), 2) == 0


def either(body, when_even):
    even = is_even()
    pl.when(even)(lambda: body(when_even))
    pl.when(jnp.logical_not(even))(lambda: body(not when_even))


def row_of(ref, start, count, rows):
    return ref[pl.ds(start, count, stride=rows), :]


def pack_kernel(half, parts, state_hbm, wind_hbm, kept_ref, winds_ref, near_ref, far_ref, sems):
    fields, levels, rows, lanes = kept_ref.shape
    size = levels // parts
    lon = pl.ds(half * lanes, lanes)
    copies = []
    for p in range(parts):
        some = pl.ds(p * size, size)
        made = pltpu.make_async_copy(state_hbm.at[:, some, :, lon], kept_ref.at[:, some], sems.at[p])
        made.start()
        copies.append(made)
    winds = pltpu.make_async_copy(wind_hbm.at[:, :, lon], winds_ref, sems.at[parts])
    winds.start()
    flat = kept_ref.reshape(fields * levels * rows, lanes)
    even = is_even()
    for p, made in enumerate(copies):
        made.wait()
        here = slice(p * size, (p + 1) * size)
        for f in range(fields):
            base = (f * levels + p * size) * rows
            for r in range(2):
                for ref, start in ((near_ref, jnp.where(even, rows - 2, 0)), (far_ref, jnp.where(even, 0, rows - 2))):
                    value = row_of(flat, base + start + r, size, rows)
                    ref[r * fields + f, here] = value.astype(jnp.bfloat16)
    winds.wait()
    speed = row_of(winds_ref.reshape(levels * rows, lanes), 0, levels, rows)
    code = encode(speed)
    for ref in (near_ref, far_ref):
        ref[2 * fields] = code


def pack(half, state, wind):
    fields, levels, rows, _ = state.shape
    parts = 4
    return call(
        functools.partial(pack_kernel, half, parts),
        [
            array((fields, levels, rows, LANES)),
            array((levels, rows, LANES)),
            array((2 * fields + 1, levels, LANES), jnp.bfloat16),
            array((2 * fields + 1, levels, LANES), jnp.bfloat16),
        ],
        (state, wind), ins=[HBM, HBM], scratch=[pltpu.SemaphoreType.DMA((parts + 1,))], moved=5_000_000)


def inner_kernel(kept_ref, winds_ref, out_ref):
    fields, levels, rows, lanes = kept_ref.shape
    step = 8
    flat = kept_ref.reshape(fields * levels * rows, lanes)
    winds = winds_ref.reshape(levels * rows, lanes)

    @pl.loop(0, levels // step)
    def _(i):
        base = i * (step * rows)
        faces = [face(row_of(winds, base + r, step, rows)) for r in range(2, rows - 1)]
        level = pl.multiple_of(i * step, step)
        for f in range(fields):
            q = [row_of(flat, f * levels * rows + base + r, step, rows) for r in range(rows)]
            for r, value in enumerate(rows_after(q, faces)):
                out_ref[r, f, pl.ds(level, step), :] = value


def inner(kept, winds):
    fields, levels, rows, lanes = kept.shape
    return call(
        inner_kernel, [array((rows - 4, fields, levels, lanes))], (kept, winds),
        flops=1_000_000, moved=1_000_000)[0]


def edge_kernel(near, kept_ref, winds_ref, halo_ref, out_ref, sent_ref):
    fields, levels, rows, lanes = kept_ref.shape
    step = 16
    flat = kept_ref.reshape(fields * levels * rows, lanes)
    winds = winds_ref.reshape(levels * rows, lanes)

    def body(bottom):
        first = rows - 2 if bottom else 0

        @pl.loop(0, levels // step)
        def _(i):
            base = i * (step * rows)
            here = pl.ds(pl.multiple_of(i * step, step), step)
            wide = lambda index: halo_ref[index, here, :].astype(jnp.float32)
            faces = [
                face(decode(wide(2 * fields)) if r == rows else row_of(winds, base + r, step, rows))
                for r in range(first, first + 3)
            ]
            for f in range(fields):
                own = lambda r: row_of(flat, f * levels * rows + base + r, step, rows)
                halo = [wide(f), wide(fields + f)]
                q = [own(r) for r in range(rows - 4, rows)] + halo if bottom else halo + [own(r) for r in range(4)]
                for r, value in enumerate(rows_after(q, faces)):
                    out_ref[r, f, here, :] = value
                    sent_ref[r * fields + f, here, :] = value.astype(jnp.bfloat16)

    either(body, near)


def edge(near, kept, winds, halo):
    fields, levels, _, lanes = kept.shape
    return call(
        functools.partial(edge_kernel, near),
        [array((2, fields, levels, lanes)), array((2 * fields, levels, lanes), jnp.bfloat16)],
        (kept, winds, halo), flops=1_000_000, moved=300_000)


def weights_kernel(first_ref, bias_ref, second_ref, remap_ref, first_out, second_out, split_out):
    inputs, hidden = first_ref.shape
    levels = remap_ref.shape[0]
    whole = remap_ref[...]
    r_high = whole.astype(jnp.bfloat16)
    r_low = (whole - r_high.astype(jnp.float32)).astype(jnp.bfloat16)
    for j in range(2):
        split_out[:levels, j * levels : (j + 1) * levels] = r_high
        split_out[levels:, j * levels : (j + 1) * levels] = r_low
    chunk = 256
    same = lambda d: lax.broadcasted_iota(jnp.int32, (chunk, chunk), d)
    unit = jnp.where(same(0) == same(1), 1.0, 0.0).astype(jnp.bfloat16)
    flip = lambda part: lax.dot_general(
        unit, part, (((1,), (1,)), ((), ())), preferred_element_type=jnp.float32).astype(jnp.bfloat16)
    small = unit[:LANES, :LANES]
    row = lax.broadcasted_iota(jnp.int32, (LANES, chunk), 0)
    for j in range(hidden // chunk):
        here = slice(j * chunk, (j + 1) * chunk)
        first_out[here, :inputs] = flip(first_ref[:, here])
        bias = bias_ref[:, here]
        high = bias.astype(jnp.bfloat16).astype(jnp.float32)
        middle = (bias - high).astype(jnp.bfloat16).astype(jnp.float32)
        low = bias - high - middle
        stacked = jnp.where(row == 0, high, jnp.where(row == 1, middle, jnp.where(row == 2, low, 0.0)))
        first_out[here, inputs:] = flip(stacked.astype(jnp.bfloat16))
        second_out[:, here] = lax.dot_general(
            small, second_ref[here, :], (((1,), (1,)), ((), ())),
            preferred_element_type=jnp.float32).astype(jnp.bfloat16)


def weights(w_first, bias, w_second, remap):
    inputs, hidden = w_first.shape
    levels = remap.shape[0]
    outputs = w_second.shape[1]
    return call(
        weights_kernel,
        [
            array((hidden, inputs + LANES), jnp.bfloat16),
            array((outputs, hidden), jnp.bfloat16),
            array((2 * levels, 2 * levels), jnp.bfloat16),
        ],
        (w_first, bias.reshape(1, hidden), w_second, remap), flops=50_000_000, moved=7_000_000)


def network(x, w1_ref, w2_ref, g_ref):
    hidden = w1_ref.shape[0]
    chunk = 512
    for c in range(hidden // chunk):
        here = slice(c * chunk, (c + 1) * chunk)
        v = jnp.dot(w1_ref[here, :], x, preferred_element_type=jnp.float32)
        h = 0.5 * v
        t = jnp.tanh(v * (GELU_A + GELU_B * (v * v)))
        g_ref[here, :] = (h + h * t).astype(jnp.bfloat16)
    return jnp.dot(w2_ref[...], g_ref[...], preferred_element_type=jnp.float32)


def advance(stage, half_refs, a, units, fields, levels, rows, lanes):
    mid, rim, wnd = half_refs[:3]
    step = 16
    winds = wnd.reshape(levels * rows, lanes)
    near = stage == "near"

    def body(bottom):
        if stage == "near":
            first, many = (rows - 4 if bottom else 0), 4
        elif stage == "between":
            first, many = (rows - 4 if bottom else 2), 2
        else:
            first, many = (rows - 2 if bottom else 0), 2

        @pl.loop(0, levels // step)
        def _(i):
            here = pl.ds(pl.multiple_of(i * step, step), step)
            there = pl.ds(pl.multiple_of(levels + i * step, step), step)
            base = i * (step * rows)
            wide = lambda ref, index: ref[index, here, :].astype(jnp.float32)

            def value_of(r, f):
                if r < 0:
                    return wide(half_refs[3], (r + 2) * fields + f)
                if r >= rows:
                    return wide(half_refs[3], (r - rows) * fields + f)
                if 2 <= r < rows - 2:
                    return mid[r - 2, f, here, :]
                return rim[r - (rows - 2) if bottom else r, f, here, :]

            faces = [
                face(decode(wide(half_refs[4], 2 * fields)) if r == rows else row_of(winds, base + r, step, rows))
                for r in range(first, first + many + 1)
            ]
            for f in range(fields):
                q = [value_of(r, f) for r in range(first - 2, first + many + 2)]
                for j, value in enumerate(rows_after(q, faces)):
                    u, place = units[j // 2], j % 2
                    cols = pl.ds(place * lanes, lanes)
                    high = value.astype(jnp.bfloat16)
                    a[u, f, here, cols] = high
                    a[u, f, there, cols] = (value - high.astype(jnp.float32)).astype(jnp.bfloat16)

    either(body, near)


def finish_kernel(stage, group, halves, *refs):
    days, sun, rcat, w1, w2, *refs = refs
    n = len(group)
    per = {"near": 5, "between": 3, "far": 5}[stage]
    parts = [refs[k * per : (k + 1) * per] for k in range(n)]
    refs = refs[n * per :]
    if stage != "near":
        refs = refs[n:]
    far = stage == "far"
    ready = ()
    if far:
        ready, refs = refs[: group[0]], refs[group[0] :]
        out_hbm, *refs = refs[1:] if group[0] else refs
    outs, refs = refs[:n], refs[n:]
    a, x, rem, g, *sems = refs
    fields, levels, rows, lanes = outs[0].shape
    inputs = fields * levels
    stores = []

    def store(source, target):
        made = pltpu.make_async_copy(source, target, sems[0].at[len(stores)])
        made.start()
        stores.append(made)

    for h, source in enumerate(ready):
        store(source.at[0], out_hbm.at[0, :, :, pl.ds(h * lanes, lanes)])
    row = lax.broadcasted_iota(jnp.int32, (x.shape[1] - inputs, x.shape[2]), 0)
    for u in range(x.shape[0]):
        x[u, inputs:, :] = jnp.where(row < 3, 1.0, 0.0).astype(jnp.bfloat16)

    even = is_even()
    plan = []
    for k in range(n):
        advance(stage, parts[k], a, (0, 1) if stage == "near" else (k,), fields, levels, rows, lanes)
        if stage == "near":
            plan += [(0, k, (rows - 4, 0)), (1, k, (rows - 2, 2))]
        elif stage == "between":
            plan.append((k, k, (2, rows - 4)))
        else:
            plan.append((k, k, (0, rows - 2)))

    def put(f, k, start, place, value):
        flat = outs[k].reshape(fields * levels * rows, lanes)
        flat[pl.ds(f * levels * rows + start + place, levels, stride=rows), :] = value

    for u, k, starts in plan:
        start = jnp.where(even, *starts)
        for f in range(fields):
            both = jnp.dot(rcat[...], a[u, f], preferred_element_type=jnp.float32)
            value = both[:levels] + both[levels:]
            x[u, f * levels : (f + 1) * levels, :] = value.astype(jnp.bfloat16)
            if f == 0:
                rem[u] = value
            else:
                for place in range(2):
                    put(f, k, start, place, value[:, place * lanes : (place + 1) * lanes])
    lon = pl.ds(group[-1] * lanes, lanes)
    if far:
        most = pl.ds(1, fields - 1)
        store(outs[0].at[most], out_hbm.at[most, :, :, lon])
    for u, k, starts in plan:
        start = jnp.where(even, *starts)
        half = group[k]
        net = network(x[u], w1, w2, g.at[u])
        for place in range(2):
            block = (start + place) * halves + half
            lit = days[0, 0] == block
            for i in range(1, days.shape[1]):
                lit = jnp.logical_or(lit, days[0, i] == block)
            part = slice(place * lanes, (place + 1) * lanes)
            light = [sun[r + place : r + place + 1, half * lanes : (half + 1) * lanes] for r in starts]
            light = jnp.where(even, *light) * jnp.where(lit, 1.0, 0.0)
            put(0, k, start, place, rem[u, :, part] + net[:, part] * light)
    if far and group[0] == halves - 1:
        store(outs[0].at[0], out_hbm.at[0, :, :, lon])
    for made in stores:
        made.wait()


def finish(stage, group, halves, shared, parts, outs=(), ready=(), whole=()):
    _, _, _, w1, _ = shared
    levels, rows, lanes = parts[0][2].shape
    fields = parts[0][0].shape[1]
    units = 2 if stage == "near" else len(group)
    scratch = [
        pltpu.VMEM((units, fields, 2 * levels, 2 * lanes), jnp.bfloat16),
        pltpu.VMEM((units, w1.shape[1], 2 * lanes), jnp.bfloat16),
        pltpu.VMEM((units, levels, 2 * lanes), jnp.float32),
        pltpu.VMEM((units, w1.shape[0], 2 * lanes), jnp.bfloat16),
    ]
    operands = tuple(shared) + sum((tuple(p) for p in parts), ())
    alias = {len(operands) + k: k for k in range(len(outs))}
    operands += tuple(outs) + tuple(ready) + tuple(whole)
    results = [array((fields, levels, rows, lanes))] * len(group)
    out_specs = [VMEM] * len(group)
    ins = [pl.BlockSpec(memory_space=pltpu.SMEM)] + [VMEM] * (len(operands) - 1)
    if stage == "far":
        scratch.append(pltpu.SemaphoreType.DMA((halves + 1,)))
        results = [array((fields, levels, rows, halves * lanes))] + results
        out_specs = [HBM] + out_specs
        alias = {key: value + 1 for key, value in alias.items()}
        if whole:
            ins[-1] = HBM
            alias[len(operands) - 1] = 0
    return call(
        functools.partial(finish_kernel, stage, group, halves), results, operands,
        ins=ins, out_specs=out_specs,
        scratch=scratch, alias=alias, limit=16, flops=units * 1_000_000_000, moved=6_000_000)


def swap(block, route):
    return lax.ppermute(block, "lat", route)


def step_of(state, wind, sunlight, day_list, w_first, bias, w_second, remap):
    halves = state.shape[3] // LANES
    count = lax.axis_size("lat")
    near_route = [(i, i ^ 1) for i in range(count) if i ^ 1 < count]
    far_route = [(i, j) for i in range(count) for j in ((i - 1) if i % 2 == 0 else (i + 1),) if 0 <= j < count]
    every = range(halves)
    barrier = lax.optimization_barrier
    kept, winds, far, mid, near1, near2, rim = [], [], [], [], [], [], []
    for h in every:
        k, w, near_sent, far_sent = pack(
            h, pltpu.with_memory_space_constraint(state, pltpu.HBM), pltpu.with_memory_space_constraint(wind, pltpu.HBM))
        kept.append(k)
        winds.append(w)
        far.append(swap(far_sent, far_route))
        near = swap(near_sent, near_route)
        m = inner(k, w)
        m, near = barrier((m, near))
        mid.append(m)
        near1.append(near)
        rows, near_sent = edge(True, k, w, near)
        rim.append(rows)
        near2.append(swap(near_sent, near_route))
        if h + 1 < halves:
            wind, near_sent = barrier((wind, near_sent))
    w1, w2, rcat = weights(w_first, bias, w_second, remap)
    shared = (day_list, sunlight, rcat, w1, w2)
    far_rim, far2, outs = [], [], []
    for h in every:
        rows, far_sent = edge(False, kept[h], winds[h], far[h])
        far_rim.append(rows)
        far2.append(swap(far_sent, far_route))
        near2[h], far_sent = barrier((near2[h], far_sent))
        outs += finish("near", (h,), halves, shared, [(mid[h], rim[h], winds[h], near2[h], near1[h])])
        if h + 1 < halves:
            far[h + 1], outs[h] = barrier((far[h + 1], outs[h]))
    parts = [(mid[h], far_rim[h], winds[h]) for h in every]
    outs = list(finish("between", tuple(every), halves, shared, parts, outs))
    far2[0], outs = barrier((far2[0], outs))
    ready, whole = [], ()
    for h in every:
        part = parts[h] + (far2[h], far[h])
        result, done = finish("far", (h,), halves, shared, [part], [outs[h]], ready, whole)
        if h == halves - 1:
            return result
        ready.append(done)
        whole = (result,)
        far2[h + 1], ready, whole = barrier((far2[h + 1], ready, whole))


def solution(mesh):
    placed = (
        P("member", None, "lat", None),
        P("member", "lat", None),
        P(("member", "lat"), None),
        P(("member", "lat"), None),
        P(),
        P(),
        P(),
        P(),
    )
    return jax.shard_map(
        step_of,
        mesh=mesh,
        in_specs=placed,
        out_specs=P("member", None, "lat", None),
        check_vma=False,
    )
```

```python
import functools
import jax
import jax.numpy as jnp
from jax import lax
from jax.experimental import pallas as pl
from jax.experimental.pallas import tpu as pltpu
from jax.sharding import PartitionSpec as P

LANES = 128
CODE = 80.0
GELU_A = 0.7978845608028654
GELU_B = 0.7978845608028654 * 0.044715
HBM = pl.BlockSpec(memory_space=pltpu.HBM)
VMEM = pl.BlockSpec(memory_space=pltpu.VMEM)
MIB = 1024 * 1024


def call(kernel, outs, operands, ins=None, out_specs=None, scratch=(), limit=8, flops=0, moved=0, alias=None):
    return pl.pallas_call(
        kernel,
        in_specs=ins or [VMEM] * len(operands),
        out_specs=out_specs or [VMEM] * len(outs),
        out_shape=outs,
        scratch_shapes=scratch,
        input_output_aliases=alias or {},
        compiler_params=pltpu.CompilerParams(vmem_limit_bytes=limit * MIB),
        cost_estimate=pl.CostEstimate(flops=flops, bytes_accessed=moved, transcendentals=0),
    )(*operands)


def array(shape, dtype=jnp.float32):
    return jax.ShapeDtypeStruct(shape, dtype)


def limited(ahead, behind):
    return jnp.maximum(jnp.minimum(ahead, jnp.maximum(behind, 0.0)), jnp.minimum(behind, 0.0))


def face(speed):
    size = jnp.abs(speed)
    return speed > 0.0, speed, size * (0.5 - 0.5 * size)


def rows_after(q, faces):
    diffs = [b - a for a, b in zip(q[:-1], q[1:])]
    slopes = [None] + [limited(b, a) for a, b in zip(diffs[:-1], diffs[1:])]
    fluxes = []
    for j, (mask, speed, half) in enumerate(faces):
        edge = jnp.where(mask, q[j + 1], q[j + 2])
        slope = jnp.where(mask, slopes[j + 1], slopes[j + 2])
        fluxes.append(speed * edge + half * slope)
    return [q[j + 2] - (fluxes[j + 1] - fluxes[j]) for j in range(len(faces) - 1)]


def encode(speed):
    size = jnp.exp(CODE * jnp.abs(speed))
    return jnp.where(speed < 0.0, -size, size).astype(jnp.bfloat16)


def decode(code):
    size = jnp.log(jnp.maximum(jnp.abs(code), 1.0)) * (1.0 / CODE)
    return jnp.where(code < 0.0, -size, size)


def is_even():
    return lax.rem(lax.axis_index("lat"), 2) == 0


def either(body, when_even):
    even = is_even()
    pl.when(even)(lambda: body(when_even))
    pl.when(jnp.logical_not(even))(lambda: body(not when_even))


def row_of(ref, start, count, rows):
    return ref[pl.ds(start, count, stride=rows), :]


def pack_kernel(half, parts, state_hbm, wind_hbm, kept_ref, winds_ref, near_ref, far_ref, sems):
    fields, levels, rows, lanes = kept_ref.shape
    size = levels // parts
    lon = pl.ds(half * lanes, lanes)
    copies = []
    for p in range(parts):
        some = pl.ds(p * size, size)
        made = pltpu.make_async_copy(state_hbm.at[:, some, :, lon], kept_ref.at[:, some], sems.at[p])
        made.start()
        copies.append(made)
    winds = pltpu.make_async_copy(wind_hbm.at[:, :, lon], winds_ref, sems.at[parts])
    winds.start()
    flat = kept_ref.reshape(fields * levels * rows, lanes)
    even = is_even()
    for p, made in enumerate(copies):
        made.wait()
        here = slice(p * size, (p + 1) * size)
        for f in range(fields):
            base = (f * levels + p * size) * rows
            for r in range(2):
                for ref, start in ((near_ref, jnp.where(even, rows - 2, 0)), (far_ref, jnp.where(even, 0, rows - 2))):
                    value = row_of(flat, base + start + r, size, rows)
                    ref[r * fields + f, here] = value.astype(jnp.bfloat16)
    winds.wait()
    speed = row_of(winds_ref.reshape(levels * rows, lanes), 0, levels, rows)
    code = encode(speed)
    for ref in (near_ref, far_ref):
        ref[2 * fields] = code


def pack(half, state, wind):
    fields, levels, rows, _ = state.shape
    parts = 4
    return call(
        functools.partial(pack_kernel, half, parts),
        [
            array((fields, levels, rows, LANES)),
            array((levels, rows, LANES)),
            array((2 * fields + 1, levels, LANES), jnp.bfloat16),
            array((2 * fields + 1, levels, LANES), jnp.bfloat16),
        ],
        (state, wind), ins=[HBM, HBM], scratch=[pltpu.SemaphoreType.DMA((parts + 1,))], moved=5_000_000)


def inner_kernel(kept_ref, winds_ref, out_ref):
    fields, levels, rows, lanes = kept_ref.shape
    step = 8
    flat = kept_ref.reshape(fields * levels * rows, lanes)
    winds = winds_ref.reshape(levels * rows, lanes)

    @pl.loop(0, levels // step)
    def _(i):
        base = i * (step * rows)
        faces = [face(row_of(winds, base + r, step, rows)) for r in range(2, rows - 1)]
        level = pl.multiple_of(i * step, step)
        for f in range(fields):
            q = [row_of(flat, f * levels * rows + base + r, step, rows) for r in range(rows)]
            for r, value in enumerate(rows_after(q, faces)):
                out_ref[r, f, pl.ds(level, step), :] = value


def inner(kept, winds):
    fields, levels, rows, lanes = kept.shape
    return call(
        inner_kernel, [array((rows - 4, fields, levels, lanes))], (kept, winds),
        flops=50_000_000, moved=4_000_000)[0]


def edge_kernel(near, kept_ref, winds_ref, halo_ref, out_ref, sent_ref):
    fields, levels, rows, lanes = kept_ref.shape
    step = 16
    flat = kept_ref.reshape(fields * levels * rows, lanes)
    winds = winds_ref.reshape(levels * rows, lanes)

    def body(bottom):
        first = rows - 2 if bottom else 0

        @pl.loop(0, levels // step)
        def _(i):
            base = i * (step * rows)
            here = pl.ds(pl.multiple_of(i * step, step), step)
            wide = lambda index: halo_ref[index, here, :].astype(jnp.float32)
            faces = [
                face(decode(wide(2 * fields)) if r == rows else row_of(winds, base + r, step, rows))
                for r in range(first, first + 3)
            ]
            for f in range(fields):
                own = lambda r: row_of(flat, f * levels * rows + base + r, step, rows)
                halo = [wide(f), wide(fields + f)]
                q = [own(r) for r in range(rows - 4, rows)] + halo if bottom else halo + [own(r) for r in range(4)]
                for r, value in enumerate(rows_after(q, faces)):
                    out_ref[r, f, here, :] = value
                    sent_ref[r * fields + f, here, :] = value.astype(jnp.bfloat16)

    either(body, near)


def edge(near, kept, winds, halo):
    fields, levels, _, lanes = kept.shape
    return call(
        functools.partial(edge_kernel, near),
        [array((2, fields, levels, lanes)), array((2 * fields, levels, lanes), jnp.bfloat16)],
        (kept, winds, halo), flops=25_000_000, moved=3_000_000)


def weights_kernel(first_ref, bias_ref, second_ref, remap_ref, first_out, second_out, split_out):
    inputs, hidden = first_ref.shape
    levels = remap_ref.shape[0]
    whole = remap_ref[...]
    r_high = whole.astype(jnp.bfloat16)
    r_low = (whole - r_high.astype(jnp.float32)).astype(jnp.bfloat16)
    for j in range(2):
        split_out[:levels, j * levels : (j + 1) * levels] = r_high
        split_out[levels:, j * levels : (j + 1) * levels] = r_low
    chunk = 256
    same = lambda d: lax.broadcasted_iota(jnp.int32, (chunk, chunk), d)
    unit = jnp.where(same(0) == same(1), 1.0, 0.0).astype(jnp.bfloat16)
    flip = lambda part: lax.dot_general(
        unit, part, (((1,), (1,)), ((), ())), preferred_element_type=jnp.float32).astype(jnp.bfloat16)
    small = unit[:LANES, :LANES]
    row = lax.broadcasted_iota(jnp.int32, (LANES, chunk), 0)
    for j in range(hidden // chunk):
        here = slice(j * chunk, (j + 1) * chunk)
        first_out[here, :inputs] = flip(first_ref[:, here])
        bias = bias_ref[:, here]
        high = bias.astype(jnp.bfloat16).astype(jnp.float32)
        middle = (bias - high).astype(jnp.bfloat16).astype(jnp.float32)
        low = bias - high - middle
        stacked = jnp.where(row == 0, high, jnp.where(row == 1, middle, jnp.where(row == 2, low, 0.0)))
        first_out[here, inputs:] = flip(stacked.astype(jnp.bfloat16))
        second_out[:, here] = lax.dot_general(
            small, second_ref[here, :], (((1,), (1,)), ((), ())),
            preferred_element_type=jnp.float32).astype(jnp.bfloat16)


def weights(w_first, bias, w_second, remap):
    inputs, hidden = w_first.shape
    levels = remap.shape[0]
    outputs = w_second.shape[1]
    return call(
        weights_kernel,
        [
            array((hidden, inputs + LANES), jnp.bfloat16),
            array((outputs, hidden), jnp.bfloat16),
            array((2 * levels, 2 * levels), jnp.bfloat16),
        ],
        (w_first, bias.reshape(1, hidden), w_second, remap), flops=50_000_000, moved=7_000_000)


def network(x, w1_ref, w2_ref, g_ref):
    hidden = w1_ref.shape[0]
    chunk = 512
    for c in range(hidden // chunk):
        here = slice(c * chunk, (c + 1) * chunk)
        v = jnp.dot(w1_ref[here, :], x, preferred_element_type=jnp.float32)
        h = 0.5 * v
        t = jnp.tanh(v * (GELU_A + GELU_B * (v * v)))
        g_ref[here, :] = (h + h * t).astype(jnp.bfloat16)
    return jnp.dot(w2_ref[...], g_ref[...], preferred_element_type=jnp.float32)


def advance(stage, half_refs, a, units, fields, levels, rows, lanes):
    mid, rim, wnd = half_refs[:3]
    step = 16
    winds = wnd.reshape(levels * rows, lanes)
    near = stage == "near"

    def body(bottom):
        if stage == "near":
            first, many = (rows - 4 if bottom else 0), 4
        elif stage == "between":
            first, many = (rows - 4 if bottom else 2), 2
        else:
            first, many = (rows - 2 if bottom else 0), 2

        @pl.loop(0, levels // step)
        def _(i):
            here = pl.ds(pl.multiple_of(i * step, step), step)
            there = pl.ds(pl.multiple_of(levels + i * step, step), step)
            base = i * (step * rows)
            wide = lambda ref, index: ref[index, here, :].astype(jnp.float32)

            def value_of(r, f):
                if r < 0:
                    return wide(half_refs[3], (r + 2) * fields + f)
                if r >= rows:
                    return wide(half_refs[3], (r - rows) * fields + f)
                if 2 <= r < rows - 2:
                    return mid[r - 2, f, here, :]
                return rim[r - (rows - 2) if bottom else r, f, here, :]

            faces = [
                face(decode(wide(half_refs[4], 2 * fields)) if r == rows else row_of(winds, base + r, step, rows))
                for r in range(first, first + many + 1)
            ]
            for f in range(fields):
                q = [value_of(r, f) for r in range(first - 2, first + many + 2)]
                for j, value in enumerate(rows_after(q, faces)):
                    u, place = units[j // 2], j % 2
                    cols = pl.ds(place * lanes, lanes)
                    high = value.astype(jnp.bfloat16)
                    a[u, f, here, cols] = high
                    a[u, f, there, cols] = (value - high.astype(jnp.float32)).astype(jnp.bfloat16)

    either(body, near)


def finish_kernel(stage, group, halves, *refs):
    days, sun, rcat, w1, w2, *refs = refs
    n = len(group)
    per = {"near": 5, "between": 3, "far": 5}[stage]
    parts = [refs[k * per : (k + 1) * per] for k in range(n)]
    refs = refs[n * per :]
    if stage != "near":
        refs = refs[n:]
    last = stage == "far" and group[-1] == halves - 1
    ready = ()
    if last:
        ready, refs = refs[: halves - 1], refs[halves - 1 :]
        out_hbm, *refs = refs
    outs, refs = refs[:n], refs[n:]
    a, x, rem, g, *sems = refs
    fields, levels, rows, lanes = outs[0].shape
    inputs = fields * levels
    stores = []

    def store(source, target):
        made = pltpu.make_async_copy(source, target, sems[0].at[len(stores)])
        made.start()
        stores.append(made)

    for h, source in enumerate(ready):
        store(source, out_hbm.at[:, :, :, pl.ds(h * lanes, lanes)])
    row = lax.broadcasted_iota(jnp.int32, (x.shape[1] - inputs, x.shape[2]), 0)
    for u in range(x.shape[0]):
        x[u, inputs:, :] = jnp.where(row < 3, 1.0, 0.0).astype(jnp.bfloat16)

    even = is_even()
    plan = []
    for k in range(n):
        advance(stage, parts[k], a, (0, 1) if stage == "near" else (k,), fields, levels, rows, lanes)
        if stage == "near":
            plan += [(0, k, (rows - 4, 0)), (1, k, (rows - 2, 2))]
        elif stage == "between":
            plan.append((k, k, (2, rows - 4)))
        else:
            plan.append((k, k, (0, rows - 2)))

    def put(f, k, start, place, value):
        flat = outs[k].reshape(fields * levels * rows, lanes)
        flat[pl.ds(f * levels * rows + start + place, levels, stride=rows), :] = value

    for u, k, starts in plan:
        start = jnp.where(even, *starts)
        for f in range(fields):
            both = jnp.dot(rcat[...], a[u, f], preferred_element_type=jnp.float32)
            value = both[:levels] + both[levels:]
            x[u, f * levels : (f + 1) * levels, :] = value.astype(jnp.bfloat16)
            if f == 0:
                rem[u] = value
            else:
                for place in range(2):
                    put(f, k, start, place, value[:, place * lanes : (place + 1) * lanes])
    lon = pl.ds(group[-1] * lanes, lanes)
    if last:
        most = pl.ds(1, fields - 1)
        store(outs[0].at[most], out_hbm.at[most, :, :, lon])
    for u, k, starts in plan:
        start = jnp.where(even, *starts)
        half = group[k]
        net = network(x[u], w1, w2, g.at[u])
        for place in range(2):
            block = (start + place) * halves + half
            lit = days[0, 0] == block
            for i in range(1, days.shape[1]):
                lit = jnp.logical_or(lit, days[0, i] == block)
            part = slice(place * lanes, (place + 1) * lanes)
            light = [sun[r + place : r + place + 1, half * lanes : (half + 1) * lanes] for r in starts]
            light = jnp.where(even, *light) * jnp.where(lit, 1.0, 0.0)
            put(0, k, start, place, rem[u, :, part] + net[:, part] * light)
    if last:
        store(outs[0].at[0], out_hbm.at[0, :, :, lon])
    for made in stores:
        made.wait()


def finish(stage, group, halves, shared, parts, outs=(), ready=()):
    _, _, _, w1, _ = shared
    levels, rows, lanes = parts[0][2].shape
    fields = parts[0][0].shape[1]
    units = 2 if stage == "near" else len(group)
    scratch = [
        pltpu.VMEM((units, fields, 2 * levels, 2 * lanes), jnp.bfloat16),
        pltpu.VMEM((units, w1.shape[1], 2 * lanes), jnp.bfloat16),
        pltpu.VMEM((units, levels, 2 * lanes), jnp.float32),
        pltpu.VMEM((units, w1.shape[0], 2 * lanes), jnp.bfloat16),
    ]
    operands = tuple(shared) + sum((tuple(p) for p in parts), ())
    alias = {len(operands) + k: k for k in range(len(outs))}
    operands += tuple(outs) + tuple(ready)
    results = [array((fields, levels, rows, lanes))] * len(group)
    out_specs = [VMEM] * len(group)
    if stage == "far" and group[-1] == halves - 1:
        scratch.append(pltpu.SemaphoreType.DMA((halves + 1,)))
        results = [array((fields, levels, rows, halves * lanes))] + results
        out_specs = [HBM] + out_specs
        alias = {key: value + 1 for key, value in alias.items()}
    return call(
        functools.partial(finish_kernel, stage, group, halves), results, operands,
        ins=[pl.BlockSpec(memory_space=pltpu.SMEM)] + [VMEM] * (len(operands) - 1), out_specs=out_specs,
        scratch=scratch, alias=alias, limit=16, flops=units * 1_000_000_000, moved=6_000_000)


def swap(block, route):
    return lax.ppermute(block, "lat", route)


def step_of(state, wind, sunlight, day_list, w_first, bias, w_second, remap):
    halves = state.shape[3] // LANES
    count = lax.axis_size("lat")
    near_route = [(i, i ^ 1) for i in range(count) if i ^ 1 < count]
    far_route = [(i, j) for i in range(count) for j in ((i - 1) if i % 2 == 0 else (i + 1),) if 0 <= j < count]
    every = range(halves)
    barrier = lax.optimization_barrier
    kept, winds, far, mid, near1, near2, rim = [], [], [], [], [], [], []
    for h in every:
        k, w, near_sent, far_sent = pack(
            h, pltpu.with_memory_space_constraint(state, pltpu.HBM), pltpu.with_memory_space_constraint(wind, pltpu.HBM))
        kept.append(k)
        winds.append(w)
        far.append(swap(far_sent, far_route))
        near = swap(near_sent, near_route)
        m = inner(k, w)
        m, near = barrier((m, near))
        mid.append(m)
        near1.append(near)
        rows, near_sent = edge(True, k, w, near)
        rim.append(rows)
        near2.append(swap(near_sent, near_route))
        if h + 1 < halves:
            wind, near_sent = barrier((wind, near_sent))
    w1, w2, rcat = weights(w_first, bias, w_second, remap)
    shared = (day_list, sunlight, rcat, w1, w2)
    far[0], rcat = barrier((far[0], rcat))
    far_rim, far2, outs = [], [], []
    for h in every:
        rows, far_sent = edge(False, kept[h], winds[h], far[h])
        far_rim.append(rows)
        far2.append(swap(far_sent, far_route))
        near2[h], far_sent = barrier((near2[h], far_sent))
        outs += finish("near", (h,), halves, shared, [(mid[h], rim[h], winds[h], near2[h], near1[h])])
        if h + 1 < halves:
            far[h + 1], outs[h] = barrier((far[h + 1], outs[h]))
    parts = [(mid[h], far_rim[h], winds[h]) for h in every]
    outs = list(finish("between", tuple(every), halves, shared, parts, outs))
    far2[0], outs = barrier((far2[0], outs))
    ready = []
    for h in every:
        part = parts[h] + (far2[h], far[h])
        done = finish("far", (h,), halves, shared, [part], [outs[h]], ready if h == halves - 1 else ())
        if h == halves - 1:
            return done[0]
        ready += done
        far2[h + 1], ready = barrier((far2[h + 1], ready))


def solution(mesh):
    placed = (
        P("member", None, "lat", None),
        P("member", "lat", None),
        P(("member", "lat"), None),
        P(("member", "lat"), None),
        P(),
        P(),
        P(),
        P(),
    )
    return jax.shard_map(
        step_of,
        mesh=mesh,
        in_specs=placed,
        out_specs=P("member", None, "lat", None),
        check_vma=False,
    )
```

```python
import functools
import jax
import jax.numpy as jnp
from jax import lax
from jax.experimental import pallas as pl
from jax.experimental.pallas import tpu as pltpu
from jax.sharding import PartitionSpec as P

LANES = 128
CODE = 80.0
GELU_A = 0.7978845608028654
GELU_B = 0.7978845608028654 * 0.044715
HBM = pl.BlockSpec(memory_space=pltpu.HBM)
VMEM = pl.BlockSpec(memory_space=pltpu.VMEM)
MIB = 1024 * 1024


def call(kernel, outs, operands, ins=None, out_specs=None, scratch=(), limit=8, flops=0, moved=0, alias=None):
    return pl.pallas_call(
        kernel,
        in_specs=ins or [VMEM] * len(operands),
        out_specs=out_specs or [VMEM] * len(outs),
        out_shape=outs,
        scratch_shapes=scratch,
        input_output_aliases=alias or {},
        compiler_params=pltpu.CompilerParams(vmem_limit_bytes=limit * MIB),
        cost_estimate=pl.CostEstimate(flops=flops, bytes_accessed=moved, transcendentals=0),
    )(*operands)


def array(shape, dtype=jnp.float32):
    return jax.ShapeDtypeStruct(shape, dtype)


def limited(ahead, behind):
    return jnp.maximum(jnp.minimum(ahead, jnp.maximum(behind, 0.0)), jnp.minimum(behind, 0.0))


def face(speed):
    size = jnp.abs(speed)
    return speed > 0.0, speed, size * (0.5 - 0.5 * size)


def rows_after(q, faces):
    diffs = [b - a for a, b in zip(q[:-1], q[1:])]
    slopes = [None] + [limited(b, a) for a, b in zip(diffs[:-1], diffs[1:])]
    fluxes = []
    for j, (mask, speed, half) in enumerate(faces):
        edge = jnp.where(mask, q[j + 1], q[j + 2])
        slope = jnp.where(mask, slopes[j + 1], slopes[j + 2])
        fluxes.append(speed * edge + half * slope)
    return [q[j + 2] - (fluxes[j + 1] - fluxes[j]) for j in range(len(faces) - 1)]


def encode(speed):
    size = jnp.exp(CODE * jnp.abs(speed))
    return jnp.where(speed < 0.0, -size, size).astype(jnp.bfloat16)


def decode(code):
    size = jnp.log(jnp.maximum(jnp.abs(code), 1.0)) * (1.0 / CODE)
    return jnp.where(code < 0.0, -size, size)


def is_even():
    return lax.rem(lax.axis_index("lat"), 2) == 0


def either(body, when_even):
    even = is_even()
    pl.when(even)(lambda: body(when_even))
    pl.when(jnp.logical_not(even))(lambda: body(not when_even))


def row_of(ref, start, count, rows):
    return ref[pl.ds(start, count, stride=rows), :]


def pack_kernel(half, parts, state_hbm, wind_hbm, kept_ref, winds_ref, near_ref, far_ref, sems):
    fields, levels, rows, lanes = kept_ref.shape
    size = levels // parts
    lon = pl.ds(half * lanes, lanes)
    winds = pltpu.make_async_copy(wind_hbm.at[:, :, lon], winds_ref, sems.at[parts])
    winds.start()
    copies = []
    for p in range(parts):
        some = pl.ds(p * size, size)
        made = pltpu.make_async_copy(state_hbm.at[:, some, :, lon], kept_ref.at[:, some], sems.at[p])
        made.start()
        copies.append(made)
    winds.wait()
    speed = row_of(winds_ref.reshape(levels * rows, lanes), 0, levels, rows)
    code = encode(speed)
    for ref in (near_ref, far_ref):
        ref[2 * fields] = code
    flat = kept_ref.reshape(fields * levels * rows, lanes)
    even = is_even()
    for p, made in enumerate(copies):
        made.wait()
        here = slice(p * size, (p + 1) * size)
        for f in range(fields):
            base = (f * levels + p * size) * rows
            for r in range(2):
                for ref, start in ((near_ref, jnp.where(even, rows - 2, 0)), (far_ref, jnp.where(even, 0, rows - 2))):
                    value = row_of(flat, base + start + r, size, rows)
                    ref[r * fields + f, here] = value.astype(jnp.bfloat16)


def pack(half, state, wind):
    fields, levels, rows, _ = state.shape
    parts = 8
    return call(
        functools.partial(pack_kernel, half, parts),
        [
            array((fields, levels, rows, LANES)),
            array((levels, rows, LANES)),
            array((2 * fields + 1, levels, LANES), jnp.bfloat16),
            array((2 * fields + 1, levels, LANES), jnp.bfloat16),
        ],
        (state, wind), ins=[HBM, HBM], scratch=[pltpu.SemaphoreType.DMA((parts + 1,))], moved=5_000_000)


def inner_kernel(kept_ref, winds_ref, out_ref):
    fields, levels, rows, lanes = kept_ref.shape
    step = 8
    flat = kept_ref.reshape(fields * levels * rows, lanes)
    winds = winds_ref.reshape(levels * rows, lanes)

    @pl.loop(0, levels // step)
    def _(i):
        base = i * (step * rows)
        faces = [face(row_of(winds, base + r, step, rows)) for r in range(2, rows - 1)]
        level = pl.multiple_of(i * step, step)
        for f in range(fields):
            q = [row_of(flat, f * levels * rows + base + r, step, rows) for r in range(rows)]
            for r, value in enumerate(rows_after(q, faces)):
                out_ref[r, f, pl.ds(level, step), :] = value


def inner(kept, winds):
    fields, levels, rows, lanes = kept.shape
    return call(
        inner_kernel, [array((rows - 4, fields, levels, lanes))], (kept, winds),
        flops=50_000_000, moved=4_000_000)[0]


def edge_kernel(near, kept_ref, winds_ref, halo_ref, out_ref, sent_ref):
    fields, levels, rows, lanes = kept_ref.shape
    step = 16
    flat = kept_ref.reshape(fields * levels * rows, lanes)
    winds = winds_ref.reshape(levels * rows, lanes)

    def body(bottom):
        first = rows - 2 if bottom else 0

        @pl.loop(0, levels // step)
        def _(i):
            base = i * (step * rows)
            here = pl.ds(pl.multiple_of(i * step, step), step)
            wide = lambda index: halo_ref[index, here, :].astype(jnp.float32)
            faces = [
                face(decode(wide(2 * fields)) if r == rows else row_of(winds, base + r, step, rows))
                for r in range(first, first + 3)
            ]
            for f in range(fields):
                own = lambda r: row_of(flat, f * levels * rows + base + r, step, rows)
                halo = [wide(f), wide(fields + f)]
                q = [own(r) for r in range(rows - 4, rows)] + halo if bottom else halo + [own(r) for r in range(4)]
                for r, value in enumerate(rows_after(q, faces)):
                    out_ref[r, f, here, :] = value
                    sent_ref[r * fields + f, here, :] = value.astype(jnp.bfloat16)

    either(body, near)


def edge(near, kept, winds, halo):
    fields, levels, _, lanes = kept.shape
    return call(
        functools.partial(edge_kernel, near),
        [array((2, fields, levels, lanes)), array((2 * fields, levels, lanes), jnp.bfloat16)],
        (kept, winds, halo), flops=25_000_000, moved=3_000_000)


def weights_kernel(first_ref, bias_ref, second_ref, remap_ref, first_out, second_out, split_out):
    inputs, hidden = first_ref.shape
    levels = remap_ref.shape[0]
    whole = remap_ref[...]
    r_high = whole.astype(jnp.bfloat16)
    r_low = (whole - r_high.astype(jnp.float32)).astype(jnp.bfloat16)
    for j in range(2):
        split_out[:levels, j * levels : (j + 1) * levels] = r_high
        split_out[levels:, j * levels : (j + 1) * levels] = r_low
    chunk = 256
    same = lambda d: lax.broadcasted_iota(jnp.int32, (chunk, chunk), d)
    unit = jnp.where(same(0) == same(1), 1.0, 0.0).astype(jnp.bfloat16)
    flip = lambda part: lax.dot_general(
        unit, part, (((1,), (1,)), ((), ())), preferred_element_type=jnp.float32).astype(jnp.bfloat16)
    small = unit[:LANES, :LANES]
    row = lax.broadcasted_iota(jnp.int32, (LANES, chunk), 0)
    for j in range(hidden // chunk):
        here = slice(j * chunk, (j + 1) * chunk)
        first_out[here, :inputs] = flip(first_ref[:, here])
        bias = bias_ref[:, here]
        high = bias.astype(jnp.bfloat16).astype(jnp.float32)
        middle = (bias - high).astype(jnp.bfloat16).astype(jnp.float32)
        low = bias - high - middle
        stacked = jnp.where(row == 0, high, jnp.where(row == 1, middle, jnp.where(row == 2, low, 0.0)))
        first_out[here, inputs:] = flip(stacked.astype(jnp.bfloat16))
        second_out[:, here] = lax.dot_general(
            small, second_ref[here, :], (((1,), (1,)), ((), ())),
            preferred_element_type=jnp.float32).astype(jnp.bfloat16)


def weights(w_first, bias, w_second, remap):
    inputs, hidden = w_first.shape
    levels = remap.shape[0]
    outputs = w_second.shape[1]
    return call(
        weights_kernel,
        [
            array((hidden, inputs + LANES), jnp.bfloat16),
            array((outputs, hidden), jnp.bfloat16),
            array((2 * levels, 2 * levels), jnp.bfloat16),
        ],
        (w_first, bias.reshape(1, hidden), w_second, remap), flops=50_000_000, moved=7_000_000)


def network(x, w1_ref, w2_ref, g_ref):
    hidden = w1_ref.shape[0]
    chunk = 512
    for c in range(hidden // chunk):
        here = slice(c * chunk, (c + 1) * chunk)
        v = jnp.dot(w1_ref[here, :], x, preferred_element_type=jnp.float32)
        h = 0.5 * v
        t = jnp.tanh(v * (GELU_A + GELU_B * (v * v)))
        g_ref[here, :] = (h + h * t).astype(jnp.bfloat16)
    return jnp.dot(w2_ref[...], g_ref[...], preferred_element_type=jnp.float32)


def advance(stage, half_refs, a, units, fields, levels, rows, lanes):
    mid, rim, wnd = half_refs[:3]
    step = 16
    winds = wnd.reshape(levels * rows, lanes)
    near = stage == "near"

    def body(bottom):
        if stage == "near":
            first, many = (rows - 4 if bottom else 0), 4
        elif stage == "between":
            first, many = (rows - 4 if bottom else 2), 2
        else:
            first, many = (rows - 2 if bottom else 0), 2

        @pl.loop(0, levels // step)
        def _(i):
            here = pl.ds(pl.multiple_of(i * step, step), step)
            there = pl.ds(pl.multiple_of(levels + i * step, step), step)
            base = i * (step * rows)
            wide = lambda ref, index: ref[index, here, :].astype(jnp.float32)

            def value_of(r, f):
                if r < 0:
                    return wide(half_refs[3], (r + 2) * fields + f)
                if r >= rows:
                    return wide(half_refs[3], (r - rows) * fields + f)
                if 2 <= r < rows - 2:
                    return mid[r - 2, f, here, :]
                return rim[r - (rows - 2) if bottom else r, f, here, :]

            faces = [
                face(decode(wide(half_refs[4], 2 * fields)) if r == rows else row_of(winds, base + r, step, rows))
                for r in range(first, first + many + 1)
            ]
            for f in range(fields):
                q = [value_of(r, f) for r in range(first - 2, first + many + 2)]
                for j, value in enumerate(rows_after(q, faces)):
                    u, place = units[j // 2], j % 2
                    cols = pl.ds(place * lanes, lanes)
                    high = value.astype(jnp.bfloat16)
                    a[u, f, here, cols] = high
                    a[u, f, there, cols] = (value - high.astype(jnp.float32)).astype(jnp.bfloat16)

    either(body, near)


def finish_kernel(stage, group, halves, *refs):
    days, sun, rcat, w1, w2, *refs = refs
    n = len(group)
    per = {"near": 5, "between": 3, "far": 5}[stage]
    parts = [refs[k * per : (k + 1) * per] for k in range(n)]
    refs = refs[n * per :]
    if stage != "near":
        refs = refs[n:]
    far = stage == "far"
    if far:
        out_hbm, *refs = refs
    outs, refs = refs[:n], refs[n:]
    a, x, rem, g, *sems = refs
    fields, levels, rows, lanes = outs[0].shape
    inputs = fields * levels
    stores = []

    def store(source, target):
        made = pltpu.make_async_copy(source, target, sems[0].at[len(stores)])
        made.start()
        stores.append(made)

    row = lax.broadcasted_iota(jnp.int32, (x.shape[1] - inputs, x.shape[2]), 0)
    for u in range(x.shape[0]):
        x[u, inputs:, :] = jnp.where(row < 3, 1.0, 0.0).astype(jnp.bfloat16)

    even = is_even()
    plan = []
    for k in range(n):
        advance(stage, parts[k], a, (0, 1) if stage == "near" else (k,), fields, levels, rows, lanes)
        if stage == "near":
            plan += [(0, k, (rows - 4, 0)), (1, k, (rows - 2, 2))]
        elif stage == "between":
            plan.append((k, k, (2, rows - 4)))
        else:
            plan.append((k, k, (0, rows - 2)))

    def put(f, k, start, place, value):
        flat = outs[k].reshape(fields * levels * rows, lanes)
        flat[pl.ds(f * levels * rows + start + place, levels, stride=rows), :] = value

    for u, k, starts in plan:
        start = jnp.where(even, *starts)
        for f in range(fields):
            both = jnp.dot(rcat[...], a[u, f], preferred_element_type=jnp.float32)
            value = both[:levels] + both[levels:]
            x[u, f * levels : (f + 1) * levels, :] = value.astype(jnp.bfloat16)
            if f == 0:
                rem[u] = value
            else:
                for place in range(2):
                    put(f, k, start, place, value[:, place * lanes : (place + 1) * lanes])
    most = pl.ds(1, fields - 1)
    for k in range(n if far else 0):
        store(outs[k].at[most], out_hbm.at[most, :, :, pl.ds(group[k] * lanes, lanes)])
    for u, k, starts in plan:
        start = jnp.where(even, *starts)
        half = group[k]
        net = network(x[u], w1, w2, g.at[u])
        for place in range(2):
            block = (start + place) * halves + half
            lit = days[0, 0] == block
            for i in range(1, days.shape[1]):
                lit = jnp.logical_or(lit, days[0, i] == block)
            part = slice(place * lanes, (place + 1) * lanes)
            light = [sun[r + place : r + place + 1, half * lanes : (half + 1) * lanes] for r in starts]
            light = jnp.where(even, *light) * jnp.where(lit, 1.0, 0.0)
            put(0, k, start, place, rem[u, :, part] + net[:, part] * light)
        if far:
            store(outs[k].at[0], out_hbm.at[0, :, :, pl.ds(half * lanes, lanes)])
    for made in stores:
        made.wait()


def finish(stage, group, halves, shared, parts, outs=()):
    _, _, _, w1, _ = shared
    levels, rows, lanes = parts[0][2].shape
    fields = parts[0][0].shape[1]
    units = 2 if stage == "near" else len(group)
    scratch = [
        pltpu.VMEM((units, fields, 2 * levels, 2 * lanes), jnp.bfloat16),
        pltpu.VMEM((units, w1.shape[1], 2 * lanes), jnp.bfloat16),
        pltpu.VMEM((units, levels, 2 * lanes), jnp.float32),
        pltpu.VMEM((units, w1.shape[0], 2 * lanes), jnp.bfloat16),
    ]
    operands = tuple(shared) + sum((tuple(p) for p in parts), ())
    alias = {len(operands) + k: k for k in range(len(outs))}
    operands += tuple(outs)
    results = [array((fields, levels, rows, lanes))] * len(group)
    out_specs = [VMEM] * len(group)
    if stage == "far":
        scratch.append(pltpu.SemaphoreType.DMA((2 * len(group),)))
        results = [array((fields, levels, rows, halves * lanes))] + results
        out_specs = [HBM] + out_specs
        alias = {key: value + 1 for key, value in alias.items()}
    return call(
        functools.partial(finish_kernel, stage, group, halves), results, operands,
        ins=[pl.BlockSpec(memory_space=pltpu.SMEM)] + [VMEM] * (len(operands) - 1), out_specs=out_specs,
        scratch=scratch, alias=alias, limit=16, flops=units * 1_000_000_000, moved=6_000_000)


def swap(block, route):
    return lax.ppermute(block, "lat", route)


def step_of(state, wind, sunlight, day_list, w_first, bias, w_second, remap):
    halves = state.shape[3] // LANES
    count = lax.axis_size("lat")
    near_route = [(i, i ^ 1) for i in range(count) if i ^ 1 < count]
    far_route = [(i, j) for i in range(count) for j in ((i - 1) if i % 2 == 0 else (i + 1),) if 0 <= j < count]
    every = range(halves)
    barrier = lax.optimization_barrier
    kept, winds, far, mid, near1, near2, rim = [], [], [], [], [], [], []
    for h in every:
        k, w, near_sent, far_sent = pack(
            h, pltpu.with_memory_space_constraint(state, pltpu.HBM), pltpu.with_memory_space_constraint(wind, pltpu.HBM))
        kept.append(k)
        winds.append(w)
        far.append(swap(far_sent, far_route))
        near = swap(near_sent, near_route)
        m = inner(k, w)
        m, near = barrier((m, near))
        mid.append(m)
        near1.append(near)
        rows, near_sent = edge(True, k, w, near)
        rim.append(rows)
        near2.append(swap(near_sent, near_route))
        if h + 1 < halves:
            wind, near_sent = barrier((wind, near_sent))
    w1, w2, rcat = weights(w_first, bias, w_second, remap)
    shared = (day_list, sunlight, rcat, w1, w2)
    far[0], rcat = barrier((far[0], rcat))
    far_rim, far2, outs = [], [], []
    for h in every:
        rows, far_sent = edge(False, kept[h], winds[h], far[h])
        far_rim.append(rows)
        far2.append(swap(far_sent, far_route))
        near2[h], far_sent = barrier((near2[h], far_sent))
        outs += finish("near", (h,), halves, shared, [(mid[h], rim[h], winds[h], near2[h], near1[h])])
        if h + 1 < halves:
            far[h + 1], outs[h] = barrier((far[h + 1], outs[h]))
    parts = [(mid[h], far_rim[h], winds[h]) for h in every]
    outs = list(finish("between", tuple(every), halves, shared, parts, outs))
    far2, outs = barrier((far2, outs))
    parts = [part + (far2[h], far[h]) for h, part in enumerate(parts)]
    return finish("far", tuple(every), halves, shared, parts, outs)[0]


def solution(mesh):
    placed = (
        P("member", None, "lat", None),
        P("member", "lat", None),
        P(("member", "lat"), None),
        P(("member", "lat"), None),
        P(),
        P(),
        P(),
        P(),
    )
    return jax.shard_map(
        step_of,
        mesh=mesh,
        in_specs=placed,
        out_specs=P("member", None, "lat", None),
        check_vma=False,
    )
```
